32 devices in a mesh: grp: 4 (over y, x), box: 8 (over z, core).
Axes of the slice: x: 2, y: 2, z: 4, core: 2. Of those that a mesh axis runs over, the one named last changes fastest.
Arguments:
- volume: bfloat16 [256, 8, 256], P('grp', 'box'), may hold values from 0.19921875 to 1
- apertures: bfloat16 [6, 256, 8, 256], P(None, 'grp', 'box'), may hold values from 0.09 to 1
- conductivity: bfloat16 [256, 8, 256], P('grp', 'box'), may hold values from 0.19921875 to 5
- source: float32 [256, 8, 256], P('grp', 'box'), may hold values from -8 to 8
- previous: float32 [256, 8, 256], P('grp', 'box'), may hold values from -6 to 6
- cut_flags: int32 [16, 8], replicated, may hold values from 0 to 2
- new_group: int32 [16], replicated, may hold values from 0 to 3, as said below
Outputs:
- smoothed: float32 [384, 8, 256], P('grp', 'box')
The draws below stay inside these ranges and needn't reach their ends.
Inputs may be any that keep to these rules, and one draw needn't show every extreme that they name: new_group never decreases along the layers; every boundary between consecutive groups lies at most one layer away from its place before the regrid, a multiple of 4; every group owns at least 2 and at most 6 layers, and some group exactly 6.
All inputs are finite; a program needn't handle non-finite values.
Results may differ from the reference program's by a relative error of at most 0.0007.
Values may be sent and summed in bfloat16 or wider, within the bound.
No kernel may reach another device: no remote copies, remote signals or barrier semaphores. Data moves between devices by JAX's collectives and lax.ppermute only.
A program may use at most 64 MiB of HBM per device.

```python
import math
import jax
import jax.numpy as jnp
from jax import lax

SIDE = 16
LPD = 4
SWEEPS = 3
CAPL = 6
LAYERS = 16
NZ = 256
BOX_ROWS = 2
BOX_COLS = 4
N_GRP = 4
N_BOX = 8


def draw_new_group(key, part):
    key_one, key_two = jax.random.split(jax.random.fold_in(key, 11))
    shifts = jax.random.randint(key_one, (N_GRP + 1,), -1, 2)
    chosen = jax.random.randint(key_two, (), 1, N_GRP - 1)
    boundary_ids = jnp.arange(N_GRP + 1)
    shifts = jnp.where(boundary_ids == chosen, -1, shifts)
    shifts = jnp.where(boundary_ids == chosen + 1, 1, shifts)
    shifts = jnp.where((boundary_ids == 0) | (boundary_ids == N_GRP), 0, shifts)
    bounds = boundary_ids * LPD + shifts
    interior = (boundary_ids >= 1) & (boundary_ids <= N_GRP - 1)
    layer_ids = jnp.arange(LAYERS)
    below_count = (bounds[None, :] <= layer_ids[:, None]) & interior[None, :]
    return jnp.sum(below_count.astype(jnp.int32), axis=1).astype(jnp.int32)


def draw_apertures(key, part):
    key_axis, key_high, key_low = jax.random.split(jax.random.fold_in(key, 23), 3)
    layer_axis = (jax.random.permutation(key_axis, LAYERS) % 3).astype(jnp.int32)
    full_shape = (6, NZ, N_BOX, SIDE * SIDE)
    high_values = jax.random.uniform(key_high, full_shape, jnp.float32, 0.7, 1.0)
    low_values = jax.random.uniform(key_low, full_shape, jnp.float32, 0.1, 0.2)
    face_axis = (jnp.arange(6) // 2).astype(jnp.int32)
    layer_of_row = (jnp.arange(NZ) // SIDE).astype(jnp.int32)
    row_axis = layer_axis[layer_of_row]
    dominant = face_axis[:, None] == row_axis[None, :]
    return jnp.where(dominant[:, :, None, None], high_values, low_values).astype(jnp.bfloat16)


def place_ends(result, stream_key, smallest, high):
    longest = result.shape.index(max(result.shape))
    spots = []
    for shift in (0, 1):
        where = [jax.random.randint(jax.random.fold_in(stream_key, axis), (), 0, length) for axis, length in enumerate(result.shape)]
        where[longest] = (where[longest] + shift) % result.shape[longest]
        spots.append(tuple(where))
    return result.at[spots[0]].set(smallest).at[spots[1]].set(high)


def levels(own_key, shape, cuts, low, top_value):
    gain, own = 1.0, jax.random.fold_in(own_key, 6)
    for dim, blocks in cuts:
        draws = jnp.exp(jax.random.uniform(jax.random.fold_in(own, dim), (blocks,), jnp.float32, low / len(cuts), top_value / len(cuts)))
        gain = gain * jnp.repeat(draws, shape[dim] // blocks).reshape([-1 if axis == dim else 1 for axis in range(len(shape))])
    return gain


def gaussian(key, shape, scale, limit, cuts=(), held_as=jnp.bfloat16):
    entries = jax.random.normal(key, shape, jnp.float32) * scale
    if len(cuts) > 0:
        entries = levels(key, shape, cuts, -0.22, 0.18) * entries
    return jnp.clip(entries, min=-limit, max=limit).astype(held_as)


def setup_inputs(seed: int = 0) -> dict:
    key_list = jax.random.split(jax.random.key(seed), 8)
    return {
        "volume": jnp.clip(0.19921875 + 0.80078125 * jax.random.uniform(key_list[0], (NZ, N_BOX, SIDE * SIDE), jnp.float32) ** levels(key_list[0], (NZ, N_BOX, SIDE * SIDE), ((0, 4), (1, 8)), -0.2, 0.2), 0.19921875, 1.0).astype(jnp.bfloat16),
        "apertures": draw_apertures(jax.random.fold_in(key_list[7], 71), 0),
        "conductivity": jnp.clip(jnp.exp(math.log(5.0) - 3.2227897 * jax.random.uniform(key_list[2], (NZ, N_BOX, SIDE * SIDE), jnp.float32) ** levels(key_list[2], (NZ, N_BOX, SIDE * SIDE), ((0, 4), (1, 8)), -0.2, 0.2)), 0.19921875, 5.0).astype(jnp.bfloat16),
        "source": gaussian(key_list[3], (NZ, N_BOX, SIDE * SIDE), 2.0, 8.0, ((0, 4), (1, 8)), jnp.float32),
        "previous": gaussian(key_list[4], (NZ, N_BOX, SIDE * SIDE), 1.0, 6.0, ((0, 4), (1, 8)), jnp.float32),
        "cut_flags": place_ends(jax.random.randint(key_list[5], (LAYERS, N_BOX), 0, 3), jax.random.fold_in(key_list[5], 1), 0, 2).astype(jnp.int32),
        "new_group": draw_new_group(jax.random.fold_in(key_list[7], 71), 0),
    }


SIGMA = 0.05


def to_grid(field):
    rows_total = field.shape[0]
    shaped = field.reshape(rows_total, BOX_ROWS, BOX_COLS, SIDE, SIDE)
    return shaped.transpose(0, 1, 3, 2, 4).reshape(rows_total, BOX_ROWS * SIDE, BOX_COLS * SIDE)


def from_grid(grid):
    rows_total = grid.shape[0]
    shaped = grid.reshape(rows_total, BOX_ROWS, SIDE, BOX_COLS, SIDE)
    return shaped.transpose(0, 1, 3, 2, 4).reshape(rows_total, BOX_ROWS * BOX_COLS, SIDE * SIDE)


def reference(volume, apertures, conductivity, source, previous, cut_flags, new_group):
    flag_cells = jnp.broadcast_to(jnp.repeat(cut_flags, SIDE, axis=0)[:, :, None], (NZ, N_BOX, SIDE * SIDE))
    flag_grid = to_grid(flag_cells)
    regular = flag_grid == 1
    active_cells = flag_grid != 0
    fraction = jnp.where(regular, 1.0, to_grid(volume).astype(jnp.float32))
    conduct = to_grid(conductivity).astype(jnp.float32)
    weights = [jnp.where(regular, 1.0, to_grid(apertures[face_index]).astype(jnp.float32)) * conduct for face_index in range(6)]
    diagonal = SIGMA * fraction + weights[0] + weights[1] + weights[2] + weights[3] + weights[4] + weights[5]
    forcing = fraction * to_grid(source)
    potential = to_grid(previous)
    grid_shape = potential.shape
    parity = (lax.broadcasted_iota(jnp.int32, grid_shape, 0) + lax.broadcasted_iota(jnp.int32, grid_shape, 1) + lax.broadcasted_iota(jnp.int32, grid_shape, 2)) % 2
    for sweep_index in range(SWEEPS):
        for colour in (0, 1):
            padded = jnp.pad(potential, 1)
            adjacent = (padded[:-2, 1:-1, 1:-1], padded[2:, 1:-1, 1:-1], padded[1:-1, :-2, 1:-1], padded[1:-1, 2:, 1:-1], padded[1:-1, 1:-1, :-2], padded[1:-1, 1:-1, 2:])
            gathered = forcing
            for face_index in range(6):
                gathered = gathered + weights[face_index] * adjacent[face_index]
            potential = jnp.where(active_cells & (parity == colour), gathered / diagonal, potential)
    flattened = from_grid(potential)
    group_ids = jnp.arange(N_GRP, dtype=jnp.int32)
    counts = jnp.sum((new_group[None, :] == group_ids[:, None]).astype(jnp.int32), axis=1).astype(jnp.int32)
    starts = (jnp.cumsum(counts) - counts).astype(jnp.int32)
    out_rows = jnp.arange(N_GRP * CAPL * SIDE, dtype=jnp.int32)
    owner_group = out_rows // (CAPL * SIDE)
    within = out_rows % (CAPL * SIDE)
    valid_rows = within < counts[owner_group] * SIDE
    source_rows = jnp.minimum(starts[owner_group] * SIDE + within, NZ - 1).astype(jnp.int32)
    picked = jnp.take(flattened, source_rows, axis=0)
    return jnp.where(valid_rows[:, None, None], picked, 0.0)
```

```python
import jax
import jax.numpy as jnp
from jax import lax
from jax.experimental import pallas as pl
from jax.experimental.pallas import tpu as pltpu
from jax.sharding import PartitionSpec as P

SIDE = 16
LPD = 4
SWEEPS = 3
SIGMA = 0.05
CELLS = SIDE * SIDE
ROWS = LPD * SIDE
OUT_ROWS = (LPD + 2) * SIDE
DEPTH = 2 * SWEEPS
REACH = 24
LANES = 128
XPOS = 32
COEFS = 8
RIM = COEFS * (DEPTH - 1) * SIDE + DEPTH * SIDE
CORNER = 96
F32 = jnp.float32
BF16 = jnp.bfloat16


def box_grid(box_count):
    box_rows = max(2, min(8, box_count // 4))
    return box_rows, box_count // box_rows


def split(value):
    high = value.astype(BF16)
    return high, (value - high.astype(F32)).astype(BF16)


def pack_kernel(vol, ap, cond, src, prev, flags, send_a, send_b, own_ap, own_qrp):
    group = lax.axis_index("grp")
    column = lax.axis_index("box")
    for layer in range(LPD):
        rows = pl.ds(layer * SIDE, SIDE)
        flag = flags[group * LPD + layer, column]
        regular = flag == 1
        covered = flag == 0
        inverse = 1.0 / cond[rows, :].astype(F32)
        fraction = jnp.where(regular, 1.0, vol[rows, :].astype(F32))
        q = jnp.where(covered, 1.0, (SIGMA * fraction) * inverse)
        own_qrp[0, rows, :] = q
        for half in range(2):
            cells = pl.ds(half * LANES, LANES)
            picked = pl.ds(layer * 2 * SIDE + half, SIDE, stride=2)
            before = prev[picked, :]
            scaled = fraction[:, half * LANES : (half + 1) * LANES] * inverse[:, half * LANES : (half + 1) * LANES]
            own_qrp[1, rows, cells] = jnp.where(covered, before, scaled * src[picked, :])
            own_qrp[2, rows, cells] = before
        for face in range(6):
            value = ap[face, rows, :].astype(F32)
            value = jnp.where(regular, 1.0, jnp.where(covered, 0.0, value))
            own_ap[face, rows, :] = value.astype(BF16)
    even = group % 2 == 0

    def emit(out, start):
        for face in range(6):
            out[face, :, :] = own_ap[face, pl.ds(start, REACH), :]
        for plane in range(3):
            high, low = split(own_qrp[plane, pl.ds(start, REACH), :])
            out[6 + 2 * plane, :, :] = high
            out[7 + 2 * plane, :, :] = low

    @pl.when(even)
    def _():
        emit(send_a, ROWS - REACH)
        emit(send_b, 0)

    @pl.when(jnp.logical_not(even))
    def _():
        emit(send_a, 0)
        emit(send_b, ROWS - REACH)


def corner_runs():
    runs = []
    row = 0
    for plane in range(COEFS + 1):
        reach = DEPTH - 1 if plane < COEFS else DEPTH
        for dy in range(1, reach):
            runs.append((plane, dy, reach - dy, row))
            row += reach - dy
    return runs


def turn_kernel(box_rows, box_cols, own_ap, own_qrp, from_a, from_b, *refs):
    n_rim = 3 if box_rows == 2 else 4
    turned = refs[0]
    rims = refs[1 : 1 + n_rim]
    corners = refs[1 + n_rim : -2]
    stage, corner_stage = refs[-2:]
    group = lax.axis_index("grp")
    column = lax.axis_index("box")
    even_group = group % 2 == 0
    box_x = column % box_cols
    box_y = column // box_cols
    stage[pl.ds(REACH + ROWS + REACH, LANES - REACH - ROWS - REACH), :] = jnp.zeros(
        (LANES - REACH - ROWS - REACH, CELLS), F32
    )
    for plane in range(9):
        if plane < 6:
            a = from_a[plane, :, :].astype(F32)
            b = from_b[plane, :, :].astype(F32)
            own = own_ap[plane, :, :].astype(F32)
        else:
            at = 6 + 2 * (plane - 6)
            a = from_a[at, :, :].astype(F32) + from_a[at + 1, :, :].astype(F32)
            b = from_b[at, :, :].astype(F32) + from_b[at + 1, :, :].astype(F32)
            own = own_qrp[plane - 6, :, :]
        stage[pl.ds(0, REACH), :] = jnp.where(even_group, b, a)
        stage[pl.ds(REACH, ROWS), :] = own
        stage[pl.ds(REACH + ROWS, REACH), :] = jnp.where(even_group, a, b)
        for half in range(2):
            turned[plane, pl.ds(half * LANES, LANES), :] = stage[:, pl.ds(half * LANES, LANES)].T

    def rim_y(out, high):
        for plane in range(COEFS + 1):
            reach = DEPTH - 1 if plane < COEFS else DEPTH
            start = (SIDE - reach) * SIDE if high else 0
            out[pl.ds(plane * (DEPTH - 1) * SIDE, reach * SIDE), :] = turned[
                plane, pl.ds(start, reach * SIDE), :
            ].astype(BF16)

    def rim_x(out, high):
        for plane in range(COEFS + 1):
            reach = DEPTH - 1 if plane < COEFS else DEPTH
            for i in range(reach):
                x = SIDE - reach + i if high else i
                out[pl.ds((plane * (DEPTH - 1) + i) * SIDE, SIDE), :] = turned[
                    plane, pl.ds(x, SIDE, stride=SIDE), :
                ].astype(BF16)

    def corner(out, high_y, high_x):
        for plane, dy, run, row in corner_runs():
            y = SIDE - dy if high_y else dy - 1
            x = SIDE - run if high_x else 0
            corner_stage[pl.ds(row, run), :] = turned[plane, pl.ds(y * SIDE + x, run), :]
        corner_stage[pl.ds(CORNER - 1, 1), :] = jnp.zeros((1, LANES), F32)
        out[...] = corner_stage[...].astype(BF16)

    for odd_x in (0, 1):

        @pl.when(box_x % 2 == odd_x)
        def _():
            rim_x(rims[0], odd_x == 0)
            rim_x(rims[1], odd_x == 1)

    for odd_y in (0, 1):

        @pl.when(box_y % 2 == odd_y)
        def _():
            rim_y(rims[2], odd_y == 0)
            if box_rows > 2:
                rim_y(rims[3], odd_y == 1)

        for odd_x in (0, 1):

            @pl.when((box_y % 2 == odd_y) & (box_x % 2 == odd_x))
            def _():
                corner(corners[0], odd_y == 0, odd_x == 0)
                corner(corners[1], odd_y == 0, odd_x == 1)
                if box_rows > 2:
                    corner(corners[2], odd_y == 1, odd_x == 0)
                    corner(corners[3], odd_y == 1, odd_x == 1)


def smooth_kernel(box_rows, box_cols, turned, *refs):
    n_rim = 3 if box_rows == 2 else 4
    n_corner = 2 if box_rows == 2 else 4
    rims = refs[:n_rim]
    corners = refs[n_rim : n_rim + n_corner]
    groups, out, planes, result = refs[n_rim + n_corner :]
    y_count = SIDE + DEPTH * (1 if box_rows == 2 else 2)
    low_base = y_count - DEPTH
    group = lax.axis_index("grp")
    column = lax.axis_index("box")
    box_x = column % box_cols
    box_y = column // box_cols

    for plane in range(9):
        for y in range(y_count):
            planes[plane, pl.ds(y * XPOS + SIDE, SIDE), :] = jnp.zeros((SIDE, LANES), F32)
            if y >= SIDE:
                planes[plane, pl.ds(y * XPOS, SIDE), :] = jnp.zeros((SIDE, LANES), F32)
            else:
                planes[plane, pl.ds(y * XPOS, SIDE), :] = turned[plane, pl.ds(y * SIDE, SIDE), :]

    def place_y(rim, high):
        for plane in range(COEFS + 1):
            reach = DEPTH - 1 if plane < COEFS else DEPTH
            for i in range(reach):
                y = SIDE + i if high else low_base + DEPTH - reach + i
                planes[plane, pl.ds(y * XPOS, SIDE), :] = rim[
                    pl.ds((plane * (DEPTH - 1) + i) * SIDE, SIDE), :
                ].astype(F32)

    def place_x(rim, high):
        for plane in range(COEFS + 1):
            reach = DEPTH - 1 if plane < COEFS else DEPTH
            for i in range(reach):
                x = SIDE + i if high else XPOS - reach + i
                planes[plane, pl.ds(x, SIDE, stride=XPOS), :] = rim[
                    pl.ds((plane * (DEPTH - 1) + i) * SIDE, SIDE), :
                ].astype(F32)

    def place_corner(piece, high_y, high_x):
        values = piece[...].astype(F32)
        for plane, dy, run, row in corner_runs():
            y = SIDE + dy - 1 if high_y else low_base + DEPTH - dy
            x = SIDE if high_x else XPOS - run
            planes[plane, pl.ds(y * XPOS + x, run), :] = values[row : row + run, :]

    for odd_x in (0, 1):

        @pl.when(box_x % 2 == odd_x)
        def _():
            place_x(rims[0], odd_x == 0)
            place_x(rims[1], odd_x == 1)

    for odd_y in (0, 1):

        @pl.when(box_y % 2 == odd_y)
        def _():
            place_y(rims[2], odd_y == 0)
            if box_rows > 2:
                place_y(rims[3], odd_y == 1)

        for odd_x in (0, 1):

            @pl.when((box_y % 2 == odd_y) & (box_x % 2 == odd_x))
            def _():
                place_corner(corners[0], odd_y == 0, odd_x == 0)
                place_corner(corners[1], odd_y == 0, odd_x == 1)
                if box_rows > 2:
                    place_corner(corners[2], odd_y == 1, odd_x == 0)
                    place_corner(corners[3], odd_y == 1, odd_x == 1)

    low_open = jnp.where(box_y > 0, 1.0, 0.0).astype(F32)
    high_open = jnp.where(box_y < box_rows - 1, 1.0, 0.0).astype(F32)
    for y in range(y_count):
        rows = pl.ds(y * XPOS, XPOS)
        weights = [planes[face, rows, :] for face in range(6)]
        total = planes[6, rows, :] + weights[0] + weights[1] + weights[2] + weights[3] + weights[4] + weights[5]
        inverse = 1.0 / jnp.where(total > 0.0, total, 1.0)
        for face in range(6):
            value = weights[face] * inverse
            if face == 2 and y == 0:
                value = value * low_open
            if face == 3 and y == SIDE - 1:
                value = value * high_open
            planes[face, rows, :] = value
        planes[7, rows, :] = planes[7, rows, :] * inverse

    parity = (
        lax.broadcasted_iota(jnp.int32, (XPOS, LANES), 0) + lax.broadcasted_iota(jnp.int32, (XPOS, LANES), 1)
    ) % 2
    for sweep in range(SWEEPS):
        for colour in (0, 1):
            for y in range(y_count):
                rows = pl.ds(y * XPOS, XPOS)
                here = planes[8, rows, :]
                low = planes[8, pl.ds((y - 1) % y_count * XPOS, XPOS), :]
                high = planes[8, pl.ds((y + 1) % y_count * XPOS, XPOS), :]
                gathered = (
                    planes[7, rows, :]
                    + planes[0, rows, :] * pltpu.roll(here, 1, 1)
                    + planes[1, rows, :] * pltpu.roll(here, LANES - 1, 1)
                    + planes[2, rows, :] * low
                    + planes[3, rows, :] * high
                    + planes[4, rows, :] * pltpu.roll(here, 1, 0)
                    + planes[5, rows, :] * pltpu.roll(here, XPOS - 1, 0)
                )
                planes[8, rows, :] = jnp.where(parity == (colour + y) % 2, gathered, here)

    for half in range(2):
        pieces = [planes[8, pl.ds((half * 8 + y) * XPOS, SIDE), :] for y in range(8)]
        result[pl.ds(0, LANES), pl.ds(half * LANES, LANES)] = jnp.concatenate(pieces, axis=0).T
    count = jnp.int32(0)
    first = jnp.int32(0)
    for layer in range(groups.shape[0]):
        owner = groups[layer]
        count = count + jnp.where(owner == group, 1, 0)
        first = first + jnp.where(owner < group, 1, 0)
    start = pl.multiple_of(REACH + (first - group * LPD) * SIDE, 8)
    valid = lax.broadcasted_iota(jnp.int32, (OUT_ROWS, LANES), 0) < count * SIDE
    for half in range(2):
        value = result[pl.ds(start, OUT_ROWS), pl.ds(half * LANES, LANES)]
        out[pl.ds(half, OUT_ROWS, stride=2), :] = jnp.where(valid, value, 0.0)


def swaps(count, kind):
    pairs = []
    for low in range(kind, count - 1, 2):
        pairs += [(low, low + 1), (low + 1, low)]
    return pairs


def lateral_pairs(box_rows, box_cols, kind_y, kind_x):
    move_y = dict(swaps(box_rows, kind_y)) if kind_y is not None else {i: i for i in range(box_rows)}
    move_x = dict(swaps(box_cols, kind_x)) if kind_x is not None else {i: i for i in range(box_cols)}
    return [
        (y * box_cols + x, move_y[y] * box_cols + move_x[x])
        for y in range(box_rows)
        for x in range(box_cols)
        if y in move_y and x in move_x
    ]


def vmem(count):
    return [pl.BlockSpec(memory_space=pltpu.VMEM)] * count


def per_device(volume, apertures, conductivity, source, previous, cut_flags, new_group):
    group_count = lax.axis_size("grp")
    box_rows, box_cols = box_grid(lax.axis_size("box"))
    smem = pl.BlockSpec(memory_space=pltpu.SMEM)
    piece = jax.ShapeDtypeStruct((12, REACH, CELLS), BF16)
    send_a, send_b, own_ap, own_qrp = pl.pallas_call(
        pack_kernel,
        out_shape=[
            piece,
            piece,
            jax.ShapeDtypeStruct((6, ROWS, CELLS), BF16),
            jax.ShapeDtypeStruct((3, ROWS, CELLS), F32),
        ],
        in_specs=vmem(5) + [smem],
        out_specs=vmem(4),
        name="pack",
    )(
        volume.reshape(ROWS, CELLS),
        apertures.reshape(6, ROWS, CELLS),
        conductivity.reshape(ROWS, CELLS),
        source.reshape(2 * ROWS, LANES),
        previous.reshape(2 * ROWS, LANES),
        cut_flags,
    )
    from_a = lax.ppermute(send_a, "grp", swaps(group_count, 0))
    from_b = lax.ppermute(send_b, "grp", swaps(group_count, 1))

    kinds = [(None, 0), (None, 1), (0, None), (0, 0), (0, 1)]
    if box_rows > 2:
        kinds = [(None, 0), (None, 1), (0, None), (1, None), (0, 0), (0, 1), (1, 0), (1, 1)]
    shapes = [
        jax.ShapeDtypeStruct((RIM if None in kind else CORNER, LANES), BF16) for kind in kinds
    ]
    turned, *sends = pl.pallas_call(
        lambda *refs: turn_kernel(box_rows, box_cols, *refs),
        out_shape=[jax.ShapeDtypeStruct((9, CELLS, LANES), F32)] + shapes,
        in_specs=vmem(4),
        out_specs=vmem(1 + len(kinds)),
        scratch_shapes=[pltpu.VMEM((LANES, CELLS), F32), pltpu.VMEM((CORNER, LANES), F32)],
        name="turn",
    )(own_ap, own_qrp, from_a, from_b)
    arrived = {}
    for index in sorted(range(len(kinds)), key=lambda i: (i != 2, kinds[i] == (None, 0))):
        arrived[index] = lax.ppermute(sends[index], "box", lateral_pairs(box_rows, box_cols, *kinds[index]))
    y_count = SIDE + DEPTH * (1 if box_rows == 2 else 2)
    smoothed = pl.pallas_call(
        lambda *refs: smooth_kernel(box_rows, box_cols, *refs),
        out_shape=jax.ShapeDtypeStruct((2 * OUT_ROWS, LANES), F32),
        in_specs=vmem(1 + len(kinds)) + [smem],
        out_specs=vmem(1)[0],
        scratch_shapes=[
            pltpu.VMEM((9, y_count * XPOS, LANES), F32),
            pltpu.VMEM((REACH + SIDE + OUT_ROWS, CELLS), F32),
        ],
        name="smooth",
    )(turned, *[arrived[index] for index in range(len(kinds))], new_group)
    return smoothed.reshape(OUT_ROWS, 1, CELLS)


def solution(mesh):
    in_specs = (
        P("grp", "box", None),
        P(None, "grp", "box", None),
        P("grp", "box", None),
        P("grp", "box", None),
        P("grp", "box", None),
        P(),
        P(),
    )
    out_specs = P("grp", "box", None)
    return jax.shard_map(
        per_device, mesh=mesh, in_specs=in_specs, out_specs=out_specs, check_vma=False
    )
```

```python
import jax
import jax.numpy as jnp
from jax import lax
from jax.experimental import pallas as pl
from jax.experimental.pallas import tpu as pltpu
from jax.sharding import PartitionSpec as P

SIDE = 16
LPD = 4
SWEEPS = 3
SIGMA = 0.05
CELLS = SIDE * SIDE
ROWS = LPD * SIDE
OUT_ROWS = (LPD + 2) * SIDE
DEPTH = 2 * SWEEPS
REACH = 24
LANES = 128
XPOS = 32
COEFS = 8
RIM = COEFS * (DEPTH - 1) * SIDE + DEPTH * SIDE
CORNER = 96
F32 = jnp.float32
BF16 = jnp.bfloat16


def box_grid(box_count):
    box_rows = max(2, min(8, box_count // 4))
    return box_rows, box_count // box_rows


def split(value):
    high = value.astype(BF16)
    return high, (value - high.astype(F32)).astype(BF16)


def cell_planes(start, count, flag, vol, ap, cond, src, prev, put):
    rows = pl.ds(start, count)
    regular = flag == 1
    covered = flag == 0
    inverse = 1.0 / cond[rows, :].astype(F32)
    fraction = jnp.where(regular, 1.0, vol[rows, :].astype(F32))
    for face in range(6):
        value = ap[face, rows, :].astype(F32)
        put(face, slice(None), jnp.where(regular, 1.0, jnp.where(covered, 0.0, value)))
    put(6, slice(None), jnp.where(covered, 1.0, (SIGMA * fraction) * inverse))
    scale = fraction * inverse
    for half in range(2):
        cells = slice(half * LANES, (half + 1) * LANES)
        picked = pl.ds(2 * start + half, count, stride=2)
        before = prev[picked, :]
        put(7, cells, jnp.where(covered, before, scale[:, cells] * src[picked, :]))
        put(8, cells, before)


def pack_kernel(vol, ap, cond, src, prev, flags, send_a, send_b):
    group = lax.axis_index("grp")
    column = lax.axis_index("box")

    def emit(out, first):
        for layer in range(LPD):
            low, high = max(layer * SIDE, first), min((layer + 1) * SIDE, first + REACH)
            if low >= high:
                continue
            rows = pl.ds(low - first, high - low)

            def put(plane, cells, value, rows=rows):
                if plane < 6:
                    out[plane, rows, cells] = value.astype(BF16)
                else:
                    at = 6 + 2 * (plane - 6)
                    out[at, rows, cells], out[at + 1, rows, cells] = split(value)

            cell_planes(low, high - low, flags[column, group * LPD + layer], vol, ap, cond, src, prev, put)

    for odd in (0, 1):

        @pl.when(group % 2 == odd)
        def _():
            emit(send_a, 0 if odd else ROWS - REACH)
            emit(send_b, ROWS - REACH if odd else 0)


def own_kernel(vol, ap, cond, src, prev, flags, own):
    group = lax.axis_index("grp")
    column = lax.axis_index("box")
    for layer in range(LPD):

        def put(plane, cells, value, rows=pl.ds(layer * SIDE, SIDE)):
            own[plane, rows, cells] = value

        cell_planes(layer * SIDE, SIDE, flags[column, group * LPD + layer], vol, ap, cond, src, prev, put)


def corner_runs():
    runs = []
    row = 0
    for plane in range(COEFS + 1):
        reach = DEPTH - 1 if plane < COEFS else DEPTH
        for dy in range(1, reach):
            runs.append((plane, dy, reach - dy, row))
            row += reach - dy
    return runs


def turn_kernel(box_rows, box_cols, own, from_a, from_b, turned, *refs):
    rims, stage = refs[:-1], refs[-1]
    even_group = lax.axis_index("grp") % 2 == 0
    box_y = lax.axis_index("box") // box_cols
    used = REACH + ROWS + REACH
    stage[pl.ds(used, LANES - used), :] = jnp.zeros((LANES - used, CELLS), F32)
    for plane in range(9):
        if plane < 6:
            a = from_a[plane, :, :].astype(F32)
            b = from_b[plane, :, :].astype(F32)
        else:
            at = 6 + 2 * (plane - 6)
            a = from_a[at, :, :].astype(F32) + from_a[at + 1, :, :].astype(F32)
            b = from_b[at, :, :].astype(F32) + from_b[at + 1, :, :].astype(F32)
        stage[pl.ds(0, REACH), :] = jnp.where(even_group, b, a)
        stage[pl.ds(REACH, ROWS), :] = own[plane, :, :]
        stage[pl.ds(REACH + ROWS, REACH), :] = jnp.where(even_group, a, b)
        for half in range(2):
            turned[plane, pl.ds(half * LANES, LANES), :] = stage[:, pl.ds(half * LANES, LANES)].T

    def rim(out, high):
        for plane in range(COEFS + 1):
            reach = DEPTH - 1 if plane < COEFS else DEPTH
            start = (SIDE - reach) * SIDE if high else 0
            out[pl.ds(plane * (DEPTH - 1) * SIDE, reach * SIDE), :] = turned[
                plane, pl.ds(start, reach * SIDE), :
            ].astype(BF16)

    for odd in (0, 1):

        @pl.when(box_y % 2 == odd)
        def _():
            for kind, out in enumerate(rims):
                rim(out, odd == kind)


def rims_kernel(box_rows, box_cols, turned, *refs):
    rims, corners, stage = refs[:2], refs[2:-1], refs[-1]
    box_x = lax.axis_index("box") % box_cols
    box_y = lax.axis_index("box") // box_cols

    def rim(out, high):
        for plane in range(COEFS + 1):
            reach = DEPTH - 1 if plane < COEFS else DEPTH
            for i in range(reach):
                x = SIDE - reach + i if high else i
                out[pl.ds((plane * (DEPTH - 1) + i) * SIDE, SIDE), :] = turned[
                    plane, pl.ds(x, SIDE, stride=SIDE), :
                ].astype(BF16)

    def corner(out, high_y, high_x):
        for plane, dy, run, row in corner_runs():
            y = SIDE - dy if high_y else dy - 1
            x = SIDE - run if high_x else 0
            stage[pl.ds(row, run), :] = turned[plane, pl.ds(y * SIDE + x, run), :]
        stage[pl.ds(CORNER - 1, 1), :] = jnp.zeros((1, LANES), F32)
        out[...] = stage[...].astype(BF16)

    for odd_x in (0, 1):

        @pl.when(box_x % 2 == odd_x)
        def _():
            rim(rims[0], odd_x == 0)
            rim(rims[1], odd_x == 1)

        for odd_y in (0, 1):

            @pl.when((box_y % 2 == odd_y) & (box_x % 2 == odd_x))
            def _():
                for index, out in enumerate(corners):
                    corner(out, odd_y == index // 2, odd_x == index % 2)


def normal(values):
    total = values[6]
    for face in range(6):
        total = total + values[face]
    inverse = 1.0 / jnp.where(total > 0.0, total, 1.0)
    return [values[face] * inverse for face in range(6)] + [values[7] * inverse]


def rows_of(box_rows):
    return SIDE + DEPTH * (1 if box_rows == 2 else 2)


def prepare_kernel(box_rows, box_cols, turned, planes):
    box_y = lax.axis_index("box") // box_cols
    low_open = jnp.where(box_y > 0, 1.0, 0.0).astype(F32)
    high_open = jnp.where(box_y < box_rows - 1, 1.0, 0.0).astype(F32)
    for y in range(rows_of(box_rows)):
        clear = pl.ds(y * XPOS + SIDE, SIDE) if y < SIDE else pl.ds(y * XPOS, XPOS)
        for plane in range(COEFS):
            planes[plane, clear, :] = jnp.zeros((SIDE if y < SIDE else XPOS, LANES), F32)
        if y >= SIDE:
            continue
        values = [turned[plane, pl.ds(y * SIDE, SIDE), :] for plane in range(COEFS)]
        weights = normal(values)
        if y == 0:
            weights[2] = weights[2] * low_open
        if y == SIDE - 1:
            weights[3] = weights[3] * high_open
        for plane, value in enumerate(weights + [turned[8, pl.ds(y * SIDE, SIDE), :]]):
            planes[plane, pl.ds(y * XPOS, SIDE), :] = value


def smooth_kernel(box_rows, box_cols, kinds, planes_in, *refs):
    pieces = dict(zip(kinds, refs[: len(kinds)], strict=True))
    groups, out, planes, result = refs[len(kinds) :]
    y_count = rows_of(box_rows)
    low_base = y_count - DEPTH
    group = lax.axis_index("grp")
    box_x = lax.axis_index("box") % box_cols
    box_y = lax.axis_index("box") // box_cols

    def place_y(rim, high):
        for i in range(DEPTH - 1):
            values = [
                rim[pl.ds((plane * (DEPTH - 1) + i) * SIDE, SIDE), :].astype(F32) for plane in range(COEFS)
            ]
            rows = pl.ds((SIDE + i if high else low_base + 1 + i) * XPOS, SIDE)
            for plane, value in enumerate(normal(values)):
                planes[plane, rows, :] = value
        for i in range(DEPTH):
            rows = pl.ds((SIDE + i if high else low_base + i) * XPOS, SIDE)
            planes[7, rows, :] = rim[pl.ds((COEFS * (DEPTH - 1) + i) * SIDE, SIDE), :].astype(F32)

    def place_x(rim, high):
        for i in range(DEPTH - 1):
            values = [
                rim[pl.ds((plane * (DEPTH - 1) + i) * SIDE, SIDE), :].astype(F32) for plane in range(COEFS)
            ]
            rows = pl.ds(SIDE + i if high else XPOS - DEPTH + 1 + i, SIDE, stride=XPOS)
            for plane, value in enumerate(normal(values)):
                planes[plane, rows, :] = value
        for i in range(DEPTH):
            rows = pl.ds(SIDE + i if high else XPOS - DEPTH + i, SIDE, stride=XPOS)
            planes[7, rows, :] = rim[pl.ds((COEFS * (DEPTH - 1) + i) * SIDE, SIDE), :].astype(F32)

    def place_corner(piece, high_y, high_x):
        cells = piece[...].astype(F32)
        found = {}
        for plane, dy, run, row in corner_runs():
            found[plane, dy] = cells[row : row + run, :]
        for dy in range(1, DEPTH):
            y = SIDE + dy - 1 if high_y else low_base + DEPTH - dy
            run = DEPTH - 1 - dy
            if run > 0:
                rows = pl.ds(y * XPOS + (SIDE if high_x else XPOS - run), run)
                for plane, value in enumerate(normal([found[plane, dy] for plane in range(COEFS)])):
                    planes[plane, rows, :] = value
            rows = pl.ds(y * XPOS + (SIDE if high_x else XPOS - run - 1), run + 1)
            planes[7, rows, :] = found[COEFS, dy]

    for odd_x in (0, 1):

        @pl.when(box_x % 2 == odd_x)
        def _():
            place_x(pieces[None, 0], odd_x == 0)
            place_x(pieces[None, 1], odd_x == 1)

    for odd_y in (0, 1):

        @pl.when(box_y % 2 == odd_y)
        def _():
            for (kind_y, kind_x), piece in pieces.items():
                if kind_x is None:
                    place_y(piece, odd_y == kind_y)

        for odd_x in (0, 1):

            @pl.when((box_y % 2 == odd_y) & (box_x % 2 == odd_x))
            def _():
                for (kind_y, kind_x), piece in pieces.items():
                    if None not in (kind_y, kind_x):
                        place_corner(piece, odd_y == kind_y, odd_x == kind_x)

    parity = (
        lax.broadcasted_iota(jnp.int32, (XPOS, LANES), 0) + lax.broadcasted_iota(jnp.int32, (XPOS, LANES), 1)
    ) % 2
    for sweep in range(SWEEPS):
        for colour in (0, 1):
            for y in range(y_count):
                rows = pl.ds(y * XPOS, XPOS)
                here = planes[7, rows, :]
                low = planes[7, pl.ds((y - 1) % y_count * XPOS, XPOS), :]
                high = planes[7, pl.ds((y + 1) % y_count * XPOS, XPOS), :]
                gathered = (
                    planes[6, rows, :]
                    + planes[0, rows, :] * pltpu.roll(here, 1, 1)
                    + planes[1, rows, :] * pltpu.roll(here, LANES - 1, 1)
                    + planes[2, rows, :] * low
                    + planes[3, rows, :] * high
                    + planes[4, rows, :] * pltpu.roll(here, 1, 0)
                    + planes[5, rows, :] * pltpu.roll(here, XPOS - 1, 0)
                )
                planes[7, rows, :] = jnp.where(parity == (colour + y) % 2, gathered, here)

    for half in range(2):
        pieces = [planes[7, pl.ds((half * 8 + y) * XPOS, SIDE), :] for y in range(8)]
        result[pl.ds(0, LANES), pl.ds(half * LANES, LANES)] = jnp.concatenate(pieces, axis=0).T
    count = jnp.int32(0)
    first = jnp.int32(0)
    for layer in range(groups.shape[0]):
        owner = groups[layer]
        count = count + jnp.where(owner == group, 1, 0)
        first = first + jnp.where(owner < group, 1, 0)
    start = pl.multiple_of(REACH + (first - group * LPD) * SIDE, 8)
    valid = lax.broadcasted_iota(jnp.int32, (OUT_ROWS, LANES), 0) < count * SIDE
    for half in range(2):
        value = result[pl.ds(start, OUT_ROWS), pl.ds(half * LANES, LANES)]
        out[pl.ds(half, OUT_ROWS, stride=2), :] = jnp.where(valid, value, 0.0)


def swaps(count, kind):
    pairs = []
    for low in range(kind, count - 1, 2):
        pairs += [(low, low + 1), (low + 1, low)]
    return pairs


def lateral_pairs(box_rows, box_cols, kind_y, kind_x):
    move_y = dict(swaps(box_rows, kind_y)) if kind_y is not None else {i: i for i in range(box_rows)}
    move_x = dict(swaps(box_cols, kind_x)) if kind_x is not None else {i: i for i in range(box_cols)}
    return [
        (y * box_cols + x, move_y[y] * box_cols + move_x[x])
        for y in range(box_rows)
        for x in range(box_cols)
        if y in move_y and x in move_x
    ]


def vmem(count):
    return [pl.BlockSpec(memory_space=pltpu.VMEM)] * count


def held(*arrays):
    return [pltpu.with_memory_space_constraint(array, pltpu.VMEM) for array in arrays]


def params():
    return pltpu.CompilerParams(vmem_limit_bytes=16 * 2**20)


def per_device(volume, apertures, conductivity, source, previous, cut_flags, new_group):
    group_count = lax.axis_size("grp")
    box_rows, box_cols = box_grid(lax.axis_size("box"))
    smem = pl.BlockSpec(memory_space=pltpu.SMEM)
    raw = (
        volume.reshape(ROWS, CELLS),
        apertures.reshape(6, ROWS, CELLS),
        conductivity.reshape(ROWS, CELLS),
        source.reshape(2 * ROWS, LANES),
        previous.reshape(2 * ROWS, LANES),
        cut_flags.T,
    )
    send_a, send_b = pl.pallas_call(
        pack_kernel,
        out_shape=[pltpu.VMEM((12, REACH, CELLS), BF16)] * 2,
        in_specs=vmem(5) + [smem],
        out_specs=vmem(2),
        compiler_params=params(),
        name="pack",
    )(*raw)
    from_a = lax.ppermute(send_a, "grp", swaps(group_count, 0))
    from_b = lax.ppermute(send_b, "grp", swaps(group_count, 1))
    own = pl.pallas_call(
        own_kernel,
        out_shape=pltpu.VMEM((9, ROWS, CELLS), F32),
        in_specs=vmem(5) + [smem],
        out_specs=vmem(1)[0],
        compiler_params=params(),
        cost_estimate=pl.CostEstimate(flops=4 * 2**20, bytes_accessed=2**20, transcendentals=0),
        name="own",
    )(*raw)

    kinds_y = [0] if box_rows == 2 else [0, 1]
    kinds = [(kind, None) for kind in kinds_y] + [(None, 0), (None, 1)]
    kinds += [(kind_y, kind_x) for kind_y in kinds_y for kind_x in (0, 1)]
    shapes = [pltpu.VMEM((RIM if None in kind else CORNER, LANES), BF16) for kind in kinds]
    turned, *sends = pl.pallas_call(
        lambda *refs: turn_kernel(box_rows, box_cols, *refs),
        out_shape=[pltpu.VMEM((9, CELLS, LANES), F32)] + shapes[: len(kinds_y)],
        in_specs=vmem(3),
        out_specs=vmem(1 + len(kinds_y)),
        scratch_shapes=[pltpu.VMEM((LANES, CELLS), F32)],
        compiler_params=params(),
        name="turn",
    )(*held(own, from_a, from_b))
    sends += pl.pallas_call(
        lambda *refs: rims_kernel(box_rows, box_cols, *refs),
        out_shape=shapes[len(kinds_y) :],
        in_specs=vmem(1),
        out_specs=vmem(len(shapes) - len(kinds_y)),
        scratch_shapes=[pltpu.VMEM((CORNER, LANES), F32)],
        compiler_params=params(),
        cost_estimate=pl.CostEstimate(flops=2**20, bytes_accessed=2**20, transcendentals=0),
        name="rims",
    )(*held(turned))
    arrived = [
        lax.ppermute(send, "box", lateral_pairs(box_rows, box_cols, *kind))
        for send, kind in zip(sends, kinds, strict=True)
    ]
    planes_shape = (COEFS, rows_of(box_rows) * XPOS, LANES)
    planes = pl.pallas_call(
        lambda *refs: prepare_kernel(box_rows, box_cols, *refs),
        out_shape=pltpu.VMEM(planes_shape, F32),
        in_specs=vmem(1),
        out_specs=vmem(1)[0],
        compiler_params=params(),
        cost_estimate=pl.CostEstimate(flops=8 * 2**20, bytes_accessed=2**20, transcendentals=0),
        name="prepare",
    )(*held(turned))
    smoothed, _ = pl.pallas_call(
        lambda *refs: smooth_kernel(box_rows, box_cols, kinds, *refs),
        out_shape=[
            jax.ShapeDtypeStruct((2 * OUT_ROWS, LANES), F32),
            pltpu.VMEM(planes_shape, F32),
        ],
        in_specs=vmem(1 + len(kinds)) + [smem],
        out_specs=vmem(2),
        scratch_shapes=[pltpu.VMEM((REACH + SIDE + OUT_ROWS, CELLS), F32)],
        input_output_aliases={0: 1},
        compiler_params=params(),
        name="smooth",
    )(*held(planes, *arrived), new_group)
    return smoothed.reshape(OUT_ROWS, 1, CELLS)


def solution(mesh):
    in_specs = (
        P("grp", "box", None),
        P(None, "grp", "box", None),
        P("grp", "box", None),
        P("grp", "box", None),
        P("grp", "box", None),
        P(),
        P(),
    )
    out_specs = P("grp", "box", None)
    return jax.shard_map(
        per_device, mesh=mesh, in_specs=in_specs, out_specs=out_specs, check_vma=False
    )
```

```python
import jax
import jax.numpy as jnp
from jax import lax
from jax.experimental import pallas as pl
from jax.experimental.pallas import tpu as pltpu
from jax.sharding import PartitionSpec as P

SIDE = 16
LPD = 4
SWEEPS = 3
SIGMA = 0.05
CELLS = SIDE * SIDE
ROWS = LPD * SIDE
OUT_ROWS = (LPD + 2) * SIDE
DEPTH = 2 * SWEEPS
REACH = 24
LANES = 128
XPOS = 32
COEFS = 8
RIM = COEFS * (DEPTH - 1) * SIDE + DEPTH * SIDE
CORNER = 96
F32 = jnp.float32
BF16 = jnp.bfloat16


def box_grid(box_count):
    box_rows = max(2, min(8, box_count // 4))
    return box_rows, box_count // box_rows


def split(value):
    high = value.astype(BF16)
    return high, (value - high.astype(F32)).astype(BF16)


def cell_planes(start, count, flag, vol, ap, cond, src, prev, put):
    rows = pl.ds(start, count)
    regular = flag == 1
    covered = flag == 0
    inverse = 1.0 / cond[rows, :].astype(F32)
    fraction = jnp.where(regular, 1.0, vol[rows, :].astype(F32))
    for face in range(6):
        value = ap[face, rows, :].astype(F32)
        put(face, slice(None), jnp.where(regular, 1.0, jnp.where(covered, 0.0, value)))
    put(6, slice(None), jnp.where(covered, 1.0, (SIGMA * fraction) * inverse))
    scale = fraction * inverse
    for half in range(2):
        cells = slice(half * LANES, (half + 1) * LANES)
        picked = pl.ds(2 * start + half, count, stride=2)
        before = prev[picked, :]
        put(7, cells, jnp.where(covered, before, scale[:, cells] * src[picked, :]))
        put(8, cells, before)


def pack_kernel(*refs):
    sources, (send_a, send_b), copies, semaphores = refs[:6], refs[6:8], refs[8:14], refs[14]
    moves = [
        pltpu.make_async_copy(source, copy, semaphores.at[index])
        for index, (source, copy) in enumerate(zip(sources, copies, strict=True))
    ]
    for move in moves:
        move.start()
    vol, ap, cond, src, prev, flags = copies
    group = lax.axis_index("grp")
    column = lax.axis_index("box")
    for move in moves:
        move.wait()

    def emit(out, first):
        for layer in range(LPD):
            low, high = max(layer * SIDE, first), min((layer + 1) * SIDE, first + REACH)
            if low >= high:
                continue
            rows = pl.ds(low - first, high - low)

            def put(plane, cells, value, rows=rows):
                if plane < 6:
                    out[plane, rows, cells] = value.astype(BF16)
                else:
                    at = 6 + 2 * (plane - 6)
                    out[at, rows, cells], out[at + 1, rows, cells] = split(value)

            cell_planes(low, high - low, flags[column, group * LPD + layer], vol, ap, cond, src, prev, put)

    for odd in (0, 1):

        @pl.when(group % 2 == odd)
        def _():
            emit(send_a, 0 if odd else ROWS - REACH)
            emit(send_b, ROWS - REACH if odd else 0)


def own_kernel(vol, ap, cond, src, prev, flags, own):
    group = lax.axis_index("grp")
    column = lax.axis_index("box")
    for layer in range(LPD):

        def put(plane, cells, value, rows=pl.ds(layer * SIDE, SIDE)):
            own[plane, rows, cells] = value

        cell_planes(layer * SIDE, SIDE, flags[column, group * LPD + layer], vol, ap, cond, src, prev, put)


def corner_runs():
    runs = []
    row = 0
    for plane in range(COEFS + 1):
        reach = DEPTH - 1 if plane < COEFS else DEPTH
        for dy in range(1, reach):
            runs.append((plane, dy, reach - dy, row))
            row += reach - dy
    return runs


def turn_kernel(box_rows, box_cols, own, from_a, from_b, turned, *refs):
    rims, stage = refs[:-1], refs[-1]
    even_group = lax.axis_index("grp") % 2 == 0
    box_y = lax.axis_index("box") // box_cols
    used = REACH + ROWS + REACH
    stage[pl.ds(used, LANES - used), :] = jnp.zeros((LANES - used, CELLS), F32)
    for plane in range(9):
        if plane < 6:
            a = from_a[plane, :, :].astype(F32)
            b = from_b[plane, :, :].astype(F32)
        else:
            at = 6 + 2 * (plane - 6)
            a = from_a[at, :, :].astype(F32) + from_a[at + 1, :, :].astype(F32)
            b = from_b[at, :, :].astype(F32) + from_b[at + 1, :, :].astype(F32)
        stage[pl.ds(0, REACH), :] = jnp.where(even_group, b, a)
        stage[pl.ds(REACH, ROWS), :] = own[plane, :, :]
        stage[pl.ds(REACH + ROWS, REACH), :] = jnp.where(even_group, a, b)
        for half in range(2):
            turned[plane, pl.ds(half * LANES, LANES), :] = stage[:, pl.ds(half * LANES, LANES)].T

    def rim(out, high):
        for plane in range(COEFS + 1):
            reach = DEPTH - 1 if plane < COEFS else DEPTH
            start = (SIDE - reach) * SIDE if high else 0
            out[pl.ds(plane * (DEPTH - 1) * SIDE, reach * SIDE), :] = turned[
                plane, pl.ds(start, reach * SIDE), :
            ].astype(BF16)

    for odd in (0, 1):

        @pl.when(box_y % 2 == odd)
        def _():
            for kind, out in enumerate(rims):
                rim(out, odd == kind)


def rims_kernel(box_rows, box_cols, turned, *refs):
    rims, corners, stage = refs[:2], refs[2:-1], refs[-1]
    box_x = lax.axis_index("box") % box_cols
    box_y = lax.axis_index("box") // box_cols

    def rim(out, high):
        for plane in range(COEFS + 1):
            reach = DEPTH - 1 if plane < COEFS else DEPTH
            for i in range(reach):
                x = SIDE - reach + i if high else i
                out[pl.ds((plane * (DEPTH - 1) + i) * SIDE, SIDE), :] = turned[
                    plane, pl.ds(x, SIDE, stride=SIDE), :
                ].astype(BF16)

    def corner(out, high_y, high_x):
        for plane, dy, run, row in corner_runs():
            y = SIDE - dy if high_y else dy - 1
            x = SIDE - run if high_x else 0
            stage[pl.ds(row, run), :] = turned[plane, pl.ds(y * SIDE + x, run), :]
        stage[pl.ds(CORNER - 1, 1), :] = jnp.zeros((1, LANES), F32)
        out[...] = stage[...].astype(BF16)

    for odd_x in (0, 1):

        @pl.when(box_x % 2 == odd_x)
        def _():
            rim(rims[0], odd_x == 0)
            rim(rims[1], odd_x == 1)

        for odd_y in (0, 1):

            @pl.when((box_y % 2 == odd_y) & (box_x % 2 == odd_x))
            def _():
                for index, out in enumerate(corners):
                    corner(out, odd_y == index // 2, odd_x == index % 2)


def normal(values):
    total = values[6]
    for face in range(6):
        total = total + values[face]
    inverse = 1.0 / jnp.where(total > 0.0, total, 1.0)
    return [values[face] * inverse for face in range(6)] + [values[7] * inverse]


def rows_of(box_rows):
    return SIDE + DEPTH * (1 if box_rows == 2 else 2)


def prepare_kernel(box_rows, box_cols, turned, planes):
    box_y = lax.axis_index("box") // box_cols
    low_open = jnp.where(box_y > 0, 1.0, 0.0).astype(F32)
    high_open = jnp.where(box_y < box_rows - 1, 1.0, 0.0).astype(F32)
    for y in range(rows_of(box_rows)):
        clear = pl.ds(y * XPOS + SIDE, SIDE) if y < SIDE else pl.ds(y * XPOS, XPOS)
        for plane in range(COEFS):
            planes[plane, clear, :] = jnp.zeros((SIDE if y < SIDE else XPOS, LANES), F32)
        if y >= SIDE:
            continue
        values = [turned[plane, pl.ds(y * SIDE, SIDE), :] for plane in range(COEFS)]
        weights = normal(values)
        if y == 0:
            weights[2] = weights[2] * low_open
        if y == SIDE - 1:
            weights[3] = weights[3] * high_open
        for plane, value in enumerate(weights + [turned[8, pl.ds(y * SIDE, SIDE), :]]):
            planes[plane, pl.ds(y * XPOS, SIDE), :] = value


def smooth_kernel(box_rows, box_cols, kinds, planes_in, *refs):
    pieces = dict(zip(kinds, refs[: len(kinds)], strict=True))
    groups, out, planes, result = refs[len(kinds) :]
    y_count = rows_of(box_rows)
    low_base = y_count - DEPTH
    group = lax.axis_index("grp")
    box_x = lax.axis_index("box") % box_cols
    box_y = lax.axis_index("box") // box_cols

    def place_y(rim, high):
        for i in range(DEPTH - 1):
            values = [
                rim[pl.ds((plane * (DEPTH - 1) + i) * SIDE, SIDE), :].astype(F32) for plane in range(COEFS)
            ]
            rows = pl.ds((SIDE + i if high else low_base + 1 + i) * XPOS, SIDE)
            for plane, value in enumerate(normal(values)):
                planes[plane, rows, :] = value
        for i in range(DEPTH):
            rows = pl.ds((SIDE + i if high else low_base + i) * XPOS, SIDE)
            planes[7, rows, :] = rim[pl.ds((COEFS * (DEPTH - 1) + i) * SIDE, SIDE), :].astype(F32)

    def place_x(rim, high):
        for i in range(DEPTH - 1):
            values = [
                rim[pl.ds((plane * (DEPTH - 1) + i) * SIDE, SIDE), :].astype(F32) for plane in range(COEFS)
            ]
            rows = pl.ds(SIDE + i if high else XPOS - DEPTH + 1 + i, SIDE, stride=XPOS)
            for plane, value in enumerate(normal(values)):
                planes[plane, rows, :] = value
        for i in range(DEPTH):
            rows = pl.ds(SIDE + i if high else XPOS - DEPTH + i, SIDE, stride=XPOS)
            planes[7, rows, :] = rim[pl.ds((COEFS * (DEPTH - 1) + i) * SIDE, SIDE), :].astype(F32)

    def place_corner(piece, high_y, high_x):
        cells = piece[...].astype(F32)
        found = {}
        for plane, dy, run, row in corner_runs():
            found[plane, dy] = cells[row : row + run, :]
        for dy in range(1, DEPTH):
            y = SIDE + dy - 1 if high_y else low_base + DEPTH - dy
            run = DEPTH - 1 - dy
            if run > 0:
                rows = pl.ds(y * XPOS + (SIDE if high_x else XPOS - run), run)
                for plane, value in enumerate(normal([found[plane, dy] for plane in range(COEFS)])):
                    planes[plane, rows, :] = value
            rows = pl.ds(y * XPOS + (SIDE if high_x else XPOS - run - 1), run + 1)
            planes[7, rows, :] = found[COEFS, dy]

    for odd_x in (0, 1):

        @pl.when(box_x % 2 == odd_x)
        def _():
            place_x(pieces[None, 0], odd_x == 0)
            place_x(pieces[None, 1], odd_x == 1)

    for odd_y in (0, 1):

        @pl.when(box_y % 2 == odd_y)
        def _():
            for (kind_y, kind_x), piece in pieces.items():
                if kind_x is None:
                    place_y(piece, odd_y == kind_y)

        for odd_x in (0, 1):

            @pl.when((box_y % 2 == odd_y) & (box_x % 2 == odd_x))
            def _():
                for (kind_y, kind_x), piece in pieces.items():
                    if None not in (kind_y, kind_x):
                        place_corner(piece, odd_y == kind_y, odd_x == kind_x)

    parity = (
        lax.broadcasted_iota(jnp.int32, (XPOS, LANES), 0) + lax.broadcasted_iota(jnp.int32, (XPOS, LANES), 1)
    ) % 2
    for sweep in range(SWEEPS):
        for colour in (0, 1):
            for y in range(y_count):
                rows = pl.ds(y * XPOS, XPOS)
                here = planes[7, rows, :]
                low = planes[7, pl.ds((y - 1) % y_count * XPOS, XPOS), :]
                high = planes[7, pl.ds((y + 1) % y_count * XPOS, XPOS), :]
                gathered = (
                    planes[6, rows, :]
                    + planes[0, rows, :] * pltpu.roll(here, 1, 1)
                    + planes[1, rows, :] * pltpu.roll(here, LANES - 1, 1)
                    + planes[2, rows, :] * low
                    + planes[3, rows, :] * high
                    + planes[4, rows, :] * pltpu.roll(here, 1, 0)
                    + planes[5, rows, :] * pltpu.roll(here, XPOS - 1, 0)
                )
                planes[7, rows, :] = jnp.where(parity == (colour + y) % 2, gathered, here)

    for half in range(2):
        pieces = [planes[7, pl.ds((half * 8 + y) * XPOS, SIDE), :] for y in range(8)]
        result[pl.ds(0, LANES), pl.ds(half * LANES, LANES)] = jnp.concatenate(pieces, axis=0).T
    count = jnp.int32(0)
    first = jnp.int32(0)
    for layer in range(groups.shape[0]):
        owner = groups[layer]
        count = count + jnp.where(owner == group, 1, 0)
        first = first + jnp.where(owner < group, 1, 0)
    start = pl.multiple_of(REACH + (first - group * LPD) * SIDE, 8)
    valid = lax.broadcasted_iota(jnp.int32, (OUT_ROWS, LANES), 0) < count * SIDE
    for half in range(2):
        value = result[pl.ds(start, OUT_ROWS), pl.ds(half * LANES, LANES)]
        out[pl.ds(half, OUT_ROWS, stride=2), :] = jnp.where(valid, value, 0.0)


def swaps(count, kind):
    pairs = []
    for low in range(kind, count - 1, 2):
        pairs += [(low, low + 1), (low + 1, low)]
    return pairs


def lateral_pairs(box_rows, box_cols, kind_y, kind_x):
    move_y = dict(swaps(box_rows, kind_y)) if kind_y is not None else {i: i for i in range(box_rows)}
    move_x = dict(swaps(box_cols, kind_x)) if kind_x is not None else {i: i for i in range(box_cols)}
    return [
        (y * box_cols + x, move_y[y] * box_cols + move_x[x])
        for y in range(box_rows)
        for x in range(box_cols)
        if y in move_y and x in move_x
    ]


def vmem(count):
    return [pl.BlockSpec(memory_space=pltpu.VMEM)] * count


def held(*arrays):
    return [pltpu.with_memory_space_constraint(array, pltpu.VMEM) for array in arrays]


def params():
    return pltpu.CompilerParams(vmem_limit_bytes=16 * 2**20)


def per_device(volume, apertures, conductivity, source, previous, cut_flags, new_group):
    group_count = lax.axis_size("grp")
    box_rows, box_cols = box_grid(lax.axis_size("box"))
    smem = pl.BlockSpec(memory_space=pltpu.SMEM)
    raw = (
        volume.reshape(ROWS, CELLS),
        apertures.reshape(6, ROWS, CELLS),
        conductivity.reshape(ROWS, CELLS),
        source.reshape(2 * ROWS, LANES),
        previous.reshape(2 * ROWS, LANES),
        cut_flags.T,
    )
    send_a, send_b, *local = pl.pallas_call(
        pack_kernel,
        out_shape=[pltpu.VMEM((12, REACH, CELLS), BF16)] * 2
        + [pltpu.VMEM(array.shape, array.dtype) for array in raw[:-1]]
        + [pltpu.SMEM(raw[-1].shape, raw[-1].dtype)],
        in_specs=[pl.BlockSpec(memory_space=pltpu.HBM)] * 6,
        out_specs=vmem(7) + [smem],
        scratch_shapes=[pltpu.SemaphoreType.DMA((6,))],
        compiler_params=params(),
        name="pack",
    )(*[pltpu.with_memory_space_constraint(array, pltpu.HBM) for array in raw])
    from_a = lax.ppermute(send_a, "grp", swaps(group_count, 0))
    from_b = lax.ppermute(send_b, "grp", swaps(group_count, 1))
    own = pl.pallas_call(
        own_kernel,
        out_shape=pltpu.VMEM((9, ROWS, CELLS), F32),
        in_specs=vmem(5) + [smem],
        out_specs=vmem(1)[0],
        compiler_params=params(),
        cost_estimate=pl.CostEstimate(flops=4 * 2**20, bytes_accessed=2**20, transcendentals=0),
        name="own",
    )(*held(*local[:-1]), local[-1])

    kinds_y = [0] if box_rows == 2 else [0, 1]
    kinds = [(kind, None) for kind in kinds_y] + [(None, 0), (None, 1)]
    kinds += [(kind_y, kind_x) for kind_y in kinds_y for kind_x in (0, 1)]
    shapes = [pltpu.VMEM((RIM if None in kind else CORNER, LANES), BF16) for kind in kinds]
    turned, *sends = pl.pallas_call(
        lambda *refs: turn_kernel(box_rows, box_cols, *refs),
        out_shape=[pltpu.VMEM((9, CELLS, LANES), F32)] + shapes[: len(kinds_y)],
        in_specs=vmem(3),
        out_specs=vmem(1 + len(kinds_y)),
        scratch_shapes=[pltpu.VMEM((LANES, CELLS), F32)],
        compiler_params=params(),
        name="turn",
    )(*held(own, from_a, from_b))
    sends += pl.pallas_call(
        lambda *refs: rims_kernel(box_rows, box_cols, *refs),
        out_shape=shapes[len(kinds_y) :],
        in_specs=vmem(1),
        out_specs=vmem(len(shapes) - len(kinds_y)),
        scratch_shapes=[pltpu.VMEM((CORNER, LANES), F32)],
        compiler_params=params(),
        cost_estimate=pl.CostEstimate(flops=2**20, bytes_accessed=2**20, transcendentals=0),
        name="rims",
    )(*held(turned))
    arrived = [
        lax.ppermute(send, "box", lateral_pairs(box_rows, box_cols, *kind))
        for send, kind in zip(sends, kinds, strict=True)
    ]
    planes_shape = (COEFS, rows_of(box_rows) * XPOS, LANES)
    planes = pl.pallas_call(
        lambda *refs: prepare_kernel(box_rows, box_cols, *refs),
        out_shape=pltpu.VMEM(planes_shape, F32),
        in_specs=vmem(1),
        out_specs=vmem(1)[0],
        compiler_params=params(),
        cost_estimate=pl.CostEstimate(flops=8 * 2**20, bytes_accessed=2**20, transcendentals=0),
        name="prepare",
    )(*held(turned))
    smoothed, _ = pl.pallas_call(
        lambda *refs: smooth_kernel(box_rows, box_cols, kinds, *refs),
        out_shape=[
            jax.ShapeDtypeStruct((2 * OUT_ROWS, LANES), F32),
            pltpu.VMEM(planes_shape, F32),
        ],
        in_specs=vmem(1 + len(kinds)) + [smem],
        out_specs=vmem(2),
        scratch_shapes=[pltpu.VMEM((REACH + SIDE + OUT_ROWS, CELLS), F32)],
        input_output_aliases={0: 1},
        compiler_params=params(),
        name="smooth",
    )(*held(planes, *arrived), new_group)
    return smoothed.reshape(OUT_ROWS, 1, CELLS)


def solution(mesh):
    in_specs = (
        P("grp", "box", None),
        P(None, "grp", "box", None),
        P("grp", "box", None),
        P("grp", "box", None),
        P("grp", "box", None),
        P(),
        P(),
    )
    out_specs = P("grp", "box", None)
    return jax.shard_map(
        per_device, mesh=mesh, in_specs=in_specs, out_specs=out_specs, check_vma=False
    )
```

```python
import jax
import jax.numpy as jnp
from jax import lax
from jax.experimental import pallas as pl
from jax.experimental.pallas import tpu as pltpu
from jax.sharding import PartitionSpec as P

SIDE = 16
LPD = 4
SWEEPS = 3
SIGMA = 0.05
CELLS = SIDE * SIDE
ROWS = LPD * SIDE
OUT_ROWS = (LPD + 2) * SIDE
DEPTH = 2 * SWEEPS
REACH = 24
LANES = 128
XPOS = 32
COEFS = 8
RIM = COEFS * (DEPTH - 1) * SIDE + DEPTH * SIDE
CORNER = 120
F32 = jnp.float32
BF16 = jnp.bfloat16


def box_grid(box_count):
    box_rows = max(2, min(8, box_count // 4))
    return box_rows, box_count // box_rows


def split(value):
    high = value.astype(BF16)
    return high, (value - high.astype(F32)).astype(BF16)


def cell_planes(start, count, flag, vol, ap, cond, src, prev, put):
    rows = pl.ds(start, count)
    regular = flag == 1
    covered = flag == 0
    inverse = 1.0 / cond[rows, :].astype(F32)
    fraction = jnp.where(regular, 1.0, vol[rows, :].astype(F32))
    for face in range(6):
        value = ap[face, rows, :].astype(F32)
        put(face, slice(None), jnp.where(regular, 1.0, jnp.where(covered, 0.0, value)))
    put(6, slice(None), jnp.where(covered, 1.0, (SIGMA * fraction) * inverse))
    scale = fraction * inverse
    for half in range(2):
        cells = slice(half * LANES, (half + 1) * LANES)
        picked = pl.ds(2 * start + half, count, stride=2)
        before = prev[picked, :]
        put(7, cells, jnp.where(covered, before, scale[:, cells] * src[picked, :]))
        put(8, cells, before)


def pack_kernel(*refs):
    sources, (send_a, send_b), copies, semaphores = refs[:6], refs[6:8], refs[8:14], refs[14]
    moves = [
        pltpu.make_async_copy(source, copy, semaphores.at[index])
        for index, (source, copy) in enumerate(zip(sources, copies, strict=True))
    ]
    for move in moves:
        move.start()
    vol, ap, cond, src, prev, flags = copies
    group = lax.axis_index("grp")
    column = lax.axis_index("box")
    for move in moves:
        move.wait()

    def emit(out, first):
        for layer in range(LPD):
            low, high = max(layer * SIDE, first), min((layer + 1) * SIDE, first + REACH)
            if low >= high:
                continue
            rows = pl.ds(low - first, high - low)

            def put(plane, cells, value, rows=rows):
                if plane == 7:
                    out[7, rows, cells], out[9, rows, cells] = split(value)
                else:
                    out[plane, rows, cells] = value.astype(BF16)

            cell_planes(low, high - low, flags[column, group * LPD + layer], vol, ap, cond, src, prev, put)

    for odd in (0, 1):

        @pl.when(group % 2 == odd)
        def _():
            emit(send_a, 0 if odd else ROWS - REACH)
            emit(send_b, ROWS - REACH if odd else 0)


def own_kernel(vol, ap, cond, src, prev, flags, own):
    group = lax.axis_index("grp")
    column = lax.axis_index("box")
    for layer in range(LPD):

        def put(plane, cells, value, rows=pl.ds(layer * SIDE, SIDE)):
            own[plane, rows, cells] = value

        cell_planes(layer * SIDE, SIDE, flags[column, group * LPD + layer], vol, ap, cond, src, prev, put)


def corner_runs():
    runs = []
    row = 0
    for plane in range(COEFS + 1):
        reach = DEPTH - 1 if plane < COEFS else DEPTH
        for dy in range(1, DEPTH):
            run = reach - (dy + 1) // 2 * 2 + 1
            if run > 0:
                runs.append((plane, dy, run, row))
                row += run
    return runs


def turn_kernel(box_rows, box_cols, own, from_a, from_b, turned, *refs):
    rims, stage = refs[:-1], refs[-1]
    even_group = lax.axis_index("grp") % 2 == 0
    box_y = lax.axis_index("box") // box_cols
    used = REACH + ROWS + REACH
    stage[pl.ds(used, LANES - used), :] = jnp.zeros((LANES - used, CELLS), F32)
    for plane in range(9):
        a = from_a[plane, :, :].astype(F32)
        b = from_b[plane, :, :].astype(F32)
        if plane == 7:
            a = a + from_a[9, :, :].astype(F32)
            b = b + from_b[9, :, :].astype(F32)
        stage[pl.ds(0, REACH), :] = jnp.where(even_group, b, a)
        stage[pl.ds(REACH, ROWS), :] = own[plane, :, :]
        stage[pl.ds(REACH + ROWS, REACH), :] = jnp.where(even_group, a, b)
        for half in range(2):
            turned[plane, pl.ds(half * LANES, LANES), :] = stage[:, pl.ds(half * LANES, LANES)].T

    def rim(out, high):
        for plane in range(COEFS + 1):
            reach = DEPTH - 1 if plane < COEFS else DEPTH
            start = (SIDE - reach) * SIDE if high else 0
            out[pl.ds(plane * (DEPTH - 1) * SIDE, reach * SIDE), :] = turned[
                plane, pl.ds(start, reach * SIDE), :
            ].astype(BF16)

    for odd in (0, 1):

        @pl.when(box_y % 2 == odd)
        def _():
            for kind, out in enumerate(rims):
                rim(out, odd == kind)


def rims_kernel(box_rows, box_cols, turned, *refs):
    rims, corners, stage = refs[:2], refs[2:-1], refs[-1]
    box_x = lax.axis_index("box") % box_cols
    box_y = lax.axis_index("box") // box_cols

    def rim(out, high):
        for plane in range(COEFS + 1):
            reach = DEPTH - 1 if plane < COEFS else DEPTH
            for i in range(reach):
                x = SIDE - reach + i if high else i
                pair = [turned[plane, pl.ds(x + odd * SIDE, SIDE // 2, stride=2 * SIDE), :] for odd in (0, 1)]
                out[pl.ds((plane * (DEPTH - 1) + i) * SIDE, SIDE), :] = jnp.concatenate(pair, axis=0).astype(BF16)

    def corner(out, high_y, high_x):
        for plane, dy, run, row in corner_runs():
            y = SIDE - dy if high_y else dy - 1
            x = SIDE - run if high_x else 0
            stage[pl.ds(row, run), :] = turned[plane, pl.ds(y * SIDE + x, run), :]
        used = corner_runs()[-1][2] + corner_runs()[-1][3]
        stage[pl.ds(used, CORNER - used), :] = jnp.zeros((CORNER - used, LANES), F32)
        out[...] = stage[...].astype(BF16)

    for odd_x in (0, 1):

        @pl.when(box_x % 2 == odd_x)
        def _():
            rim(rims[0], odd_x == 0)
            rim(rims[1], odd_x == 1)

        for odd_y in (0, 1):

            @pl.when((box_y % 2 == odd_y) & (box_x % 2 == odd_x))
            def _():
                for index, out in enumerate(corners):
                    corner(out, odd_y == index // 2, odd_x == index % 2)


def normal(values):
    total = values[6]
    for face in range(6):
        total = total + values[face]
    inverse = 1.0 / jnp.where(total > 0.0, total, 1.0)
    return [values[face] * inverse for face in range(6)] + [values[7] * inverse]


def rows_of(box_rows):
    return SIDE + DEPTH * (1 if box_rows == 2 else 2)


def pairs_of(box_rows):
    return rows_of(box_rows) // 2


def odd_cells(count, first_x):
    shape = (count, LANES)
    cells = lax.broadcasted_iota(jnp.int32, shape, 0) + lax.broadcasted_iota(jnp.int32, shape, 1)
    return (cells + first_x) % 2 == 1


def odd_lanes(count, x):
    return (lax.broadcasted_iota(jnp.int32, (count, LANES), 1) + x) % 2 == 1


def put_pair(planes, plane, rows, odd, low, high):
    planes[0, plane, rows, :] = jnp.where(odd, high, low)
    planes[1, plane, rows, :] = jnp.where(odd, low, high)


def prepare_kernel(box_rows, box_cols, turned, planes):
    box_y = lax.axis_index("box") // box_cols
    low_open = jnp.where(box_y > 0, 1.0, 0.0).astype(F32)
    high_open = jnp.where(box_y < box_rows - 1, 1.0, 0.0).astype(F32)
    odd = odd_cells(SIDE, 0)

    def weights_at(y):
        weights = normal([turned[plane, pl.ds(y * SIDE, SIDE), :] for plane in range(COEFS)])
        if y == 0:
            weights[2] = weights[2] * low_open
        if y == SIDE - 1:
            weights[3] = weights[3] * high_open
        return weights + [turned[8, pl.ds(y * SIDE, SIDE), :]]

    for k in range(pairs_of(box_rows)):
        own = 2 * k < SIDE
        clear = pl.ds(k * XPOS + SIDE, SIDE) if own else pl.ds(k * XPOS, XPOS)
        for colour in (0, 1):
            for plane in range(COEFS):
                planes[colour, plane, clear, :] = jnp.zeros((SIDE if own else XPOS, LANES), F32)
        if own:
            for plane, (low, high) in enumerate(zip(weights_at(2 * k), weights_at(2 * k + 1), strict=True)):
                put_pair(planes, plane, pl.ds(k * XPOS, SIDE), odd, low, high)


def smooth_kernel(box_rows, box_cols, kinds, planes_in, *refs):
    pieces = dict(zip(kinds, refs[: len(kinds)], strict=True))
    groups, out, planes, result = refs[len(kinds) :]
    pair_count = pairs_of(box_rows)
    low_pair = pair_count - DEPTH // 2
    high_pair = SIDE // 2
    group = lax.axis_index("grp")
    box_x = lax.axis_index("box") % box_cols
    box_y = lax.axis_index("box") // box_cols

    def slab(rim, index):
        return rim[pl.ds(index * SIDE, SIDE), :].astype(F32)

    def place_y(rim, high):
        odd = odd_cells(SIDE, 0)
        empty = jnp.zeros((SIDE, LANES), F32)

        def weights_at(i):
            i = i if high else i - 1
            if not 0 <= i < DEPTH - 1:
                return [empty] * (COEFS - 1)
            return normal([slab(rim, plane * (DEPTH - 1) + i) for plane in range(COEFS)])

        for j in range(DEPTH // 2):
            rows = pl.ds(((high_pair if high else low_pair) + j) * XPOS, SIDE)
            two = [weights_at(2 * j + i) + [slab(rim, COEFS * (DEPTH - 1) + 2 * j + i)] for i in (0, 1)]
            for plane, (low_value, high_value) in enumerate(zip(*two, strict=True)):
                put_pair(planes, plane, rows, odd, low_value, high_value)

    def place_x(rim, high):
        half = SIDE // 2
        for i in range(DEPTH):
            x = SIDE + i if high else XPOS - DEPTH + i
            at = i if high else i - 1
            rows = pl.ds(x, half, stride=XPOS)
            odd = odd_lanes(half, x)
            if 0 <= at < DEPTH - 1:
                for plane, value in enumerate(normal([slab(rim, plane * (DEPTH - 1) + at) for plane in range(COEFS)])):
                    put_pair(planes, plane, rows, odd, value[:half], value[half:])
            value = slab(rim, COEFS * (DEPTH - 1) + i)
            put_pair(planes, 7, rows, odd, value[:half], value[half:])

    def place_corner(piece, high_y, high_x):
        cells = piece[...].astype(F32)
        found = {(plane, dy): cells[row : row + run, :] for plane, dy, run, row in corner_runs()}
        for j in range(DEPTH // 2):
            k = (high_pair + j if high_y else low_pair + DEPTH // 2 - 1 - j) * XPOS
            near = [2 * j + 1, 2 * j + 2] if high_y else [2 * j + 2, 2 * j + 1]
            groups_of = []
            if (0, near[0]) in found:
                two = [normal([found[plane, dy] for plane in range(COEFS)]) for dy in near]
                groups_of += [(plane, low, high) for plane, (low, high) in enumerate(zip(*two, strict=True))]
            if (COEFS, 2 * j + 1) in found:
                pair = [found.get((COEFS, dy), jnp.zeros_like(found[COEFS, 2 * j + 1])) for dy in near]
                groups_of.append((7, *pair))
            for plane, low, high in groups_of:
                run = low.shape[0]
                x = SIDE if high_x else XPOS - run
                put_pair(planes, plane, pl.ds(k + x, run), odd_cells(run, x), low, high)

    for odd_x in (0, 1):

        @pl.when(box_x % 2 == odd_x)
        def _():
            place_x(pieces[None, 0], odd_x == 0)
            place_x(pieces[None, 1], odd_x == 1)

    for odd_y in (0, 1):

        @pl.when(box_y % 2 == odd_y)
        def _():
            for (kind_y, kind_x), piece in pieces.items():
                if kind_x is None:
                    place_y(piece, odd_y == kind_y)

        for odd_x in (0, 1):

            @pl.when((box_y % 2 == odd_y) & (box_x % 2 == odd_x))
            def _():
                for (kind_y, kind_x), piece in pieces.items():
                    if None not in (kind_y, kind_x):
                        place_corner(piece, odd_y == kind_y, odd_x == kind_x)

    odd = odd_cells(XPOS, 0)

    def update(colour, k):
        def at(offset):
            if isinstance(k, int):
                return pl.ds((k + offset) % pair_count * XPOS, XPOS)
            return pl.ds(pl.multiple_of(lax.rem(k + (offset + pair_count), pair_count) * XPOS, XPOS), XPOS)

        here = planes[1 - colour, 7, at(0), :]
        below = planes[1 - colour, 7, at(-1), :]
        above = planes[1 - colour, 7, at(1), :]
        if colour == 0:
            low, high = jnp.where(odd, here, below), jnp.where(odd, above, here)
        else:
            low, high = jnp.where(odd, below, here), jnp.where(odd, here, above)
        adjacent = (
            pltpu.roll(here, 1, 1),
            pltpu.roll(here, LANES - 1, 1),
            low,
            high,
            pltpu.roll(here, 1, 0),
            pltpu.roll(here, XPOS - 1, 0),
        )
        gathered = planes[colour, 6, at(0), :]
        for face in range(6):
            gathered = gathered + planes[colour, face, at(0), :] * adjacent[face]
        planes[colour, 7, at(0), :] = gathered

    even_row = box_y % 2 == 0
    for half_sweep in range(2 * SWEEPS):
        colour = half_sweep % 2
        for k in range(high_pair):
            update(colour, k)
        for j in range((DEPTH - half_sweep) // 2):
            if box_rows == 2:
                update(colour, jnp.where(even_row, high_pair + j, pair_count - 1 - j))
            else:
                update(colour, high_pair + j)
                update(colour, pair_count - 1 - j)

    odd = odd_cells(SIDE, 0)
    for half in range(2):
        cells = []
        for k in range(half * 4, half * 4 + 4):
            red = planes[0, 7, pl.ds(k * XPOS, SIDE), :]
            black = planes[1, 7, pl.ds(k * XPOS, SIDE), :]
            cells += [jnp.where(odd, black, red), jnp.where(odd, red, black)]
        result[pl.ds(0, LANES), pl.ds(half * LANES, LANES)] = jnp.concatenate(cells, axis=0).T
    count = jnp.int32(0)
    first = jnp.int32(0)
    for layer in range(groups.shape[0]):
        owner = groups[layer]
        count = count + jnp.where(owner == group, 1, 0)
        first = first + jnp.where(owner < group, 1, 0)
    start = pl.multiple_of(REACH + (first - group * LPD) * SIDE, 8)
    valid = lax.broadcasted_iota(jnp.int32, (OUT_ROWS, LANES), 0) < count * SIDE
    for half in range(2):
        value = result[pl.ds(start, OUT_ROWS), pl.ds(half * LANES, LANES)]
        out[pl.ds(half, OUT_ROWS, stride=2), :] = jnp.where(valid, value, 0.0)


def swaps(count, kind):
    pairs = []
    for low in range(kind, count - 1, 2):
        pairs += [(low, low + 1), (low + 1, low)]
    return pairs


def lateral_pairs(box_rows, box_cols, kind_y, kind_x):
    move_y = dict(swaps(box_rows, kind_y)) if kind_y is not None else {i: i for i in range(box_rows)}
    move_x = dict(swaps(box_cols, kind_x)) if kind_x is not None else {i: i for i in range(box_cols)}
    return [
        (y * box_cols + x, move_y[y] * box_cols + move_x[x])
        for y in range(box_rows)
        for x in range(box_cols)
        if y in move_y and x in move_x
    ]


def vmem(count):
    return [pl.BlockSpec(memory_space=pltpu.VMEM)] * count


def held(*arrays):
    return [pltpu.with_memory_space_constraint(array, pltpu.VMEM) for array in arrays]


def params():
    return pltpu.CompilerParams(vmem_limit_bytes=16 * 2**20)


def per_device(volume, apertures, conductivity, source, previous, cut_flags, new_group):
    group_count = lax.axis_size("grp")
    box_rows, box_cols = box_grid(lax.axis_size("box"))
    smem = pl.BlockSpec(memory_space=pltpu.SMEM)
    raw = (
        volume.reshape(ROWS, CELLS),
        apertures.reshape(6, ROWS, CELLS),
        conductivity.reshape(ROWS, CELLS),
        source.reshape(2 * ROWS, LANES),
        previous.reshape(2 * ROWS, LANES),
        cut_flags.T,
    )
    send_a, send_b, *local = pl.pallas_call(
        pack_kernel,
        out_shape=[pltpu.VMEM((10, REACH, CELLS), BF16)] * 2
        + [pltpu.VMEM(array.shape, array.dtype) for array in raw[:-1]]
        + [pltpu.SMEM(raw[-1].shape, raw[-1].dtype)],
        in_specs=[pl.BlockSpec(memory_space=pltpu.HBM)] * 6,
        out_specs=vmem(7) + [smem],
        scratch_shapes=[pltpu.SemaphoreType.DMA((6,))],
        compiler_params=params(),
        name="pack",
    )(*[pltpu.with_memory_space_constraint(array, pltpu.HBM) for array in raw])
    from_a = lax.ppermute(send_a, "grp", swaps(group_count, 0))
    from_b = lax.ppermute(send_b, "grp", swaps(group_count, 1))
    own = pl.pallas_call(
        own_kernel,
        out_shape=pltpu.VMEM((9, ROWS, CELLS), F32),
        in_specs=vmem(5) + [smem],
        out_specs=vmem(1)[0],
        compiler_params=params(),
        cost_estimate=pl.CostEstimate(flops=4 * 2**20, bytes_accessed=2**20, transcendentals=0),
        name="own",
    )(*held(*local[:-1]), local[-1])

    kinds_y = [0] if box_rows == 2 else [0, 1]
    kinds = [(kind, None) for kind in kinds_y] + [(None, 0), (None, 1)]
    kinds += [(kind_y, kind_x) for kind_y in kinds_y for kind_x in (0, 1)]
    shapes = [pltpu.VMEM((RIM if None in kind else CORNER, LANES), BF16) for kind in kinds]
    turned, *sends = pl.pallas_call(
        lambda *refs: turn_kernel(box_rows, box_cols, *refs),
        out_shape=[pltpu.VMEM((9, CELLS, LANES), F32)] + shapes[: len(kinds_y)],
        in_specs=vmem(3),
        out_specs=vmem(1 + len(kinds_y)),
        scratch_shapes=[pltpu.VMEM((LANES, CELLS), F32)],
        compiler_params=params(),
        name="turn",
    )(*held(own, from_a, from_b))
    sends += pl.pallas_call(
        lambda *refs: rims_kernel(box_rows, box_cols, *refs),
        out_shape=shapes[len(kinds_y) :],
        in_specs=vmem(1),
        out_specs=vmem(len(shapes) - len(kinds_y)),
        scratch_shapes=[pltpu.VMEM((CORNER, LANES), F32)],
        compiler_params=params(),
        cost_estimate=pl.CostEstimate(flops=2**20, bytes_accessed=2**20, transcendentals=0),
        name="rims",
    )(*held(turned))
    arrived = [
        lax.ppermute(send, "box", lateral_pairs(box_rows, box_cols, *kind))
        for send, kind in zip(sends, kinds, strict=True)
    ]
    planes_shape = (2, COEFS, pairs_of(box_rows) * XPOS, LANES)
    planes = pl.pallas_call(
        lambda *refs: prepare_kernel(box_rows, box_cols, *refs),
        out_shape=pltpu.VMEM(planes_shape, F32),
        in_specs=vmem(1),
        out_specs=vmem(1)[0],
        compiler_params=params(),
        cost_estimate=pl.CostEstimate(flops=8 * 2**20, bytes_accessed=2**20, transcendentals=0),
        name="prepare",
    )(*held(turned))
    smoothed, _ = pl.pallas_call(
        lambda *refs: smooth_kernel(box_rows, box_cols, kinds, *refs),
        out_shape=[
            jax.ShapeDtypeStruct((2 * OUT_ROWS, LANES), F32),
            pltpu.VMEM(planes_shape, F32),
        ],
        in_specs=vmem(1 + len(kinds)) + [smem],
        out_specs=vmem(2),
        scratch_shapes=[pltpu.VMEM((REACH + SIDE + OUT_ROWS, CELLS), F32)],
        input_output_aliases={0: 1},
        compiler_params=params(),
        name="smooth",
    )(*held(planes, *arrived), new_group)
    return smoothed.reshape(OUT_ROWS, 1, CELLS)


def solution(mesh):
    in_specs = (
        P("grp", "box", None),
        P(None, "grp", "box", None),
        P("grp", "box", None),
        P("grp", "box", None),
        P("grp", "box", None),
        P(),
        P(),
    )
    out_specs = P("grp", "box", None)
    return jax.shard_map(
        per_device, mesh=mesh, in_specs=in_specs, out_specs=out_specs, check_vma=False
    )
```

```python
import jax
import jax.numpy as jnp
from jax import lax
from jax.experimental import pallas as pl
from jax.experimental.pallas import tpu as pltpu
from jax.sharding import PartitionSpec as P

SIDE = 16
LPD = 4
SWEEPS = 3
SIGMA = 0.05
CELLS = SIDE * SIDE
ROWS = LPD * SIDE
OUT_ROWS = (LPD + 2) * SIDE
DEPTH = 2 * SWEEPS
REACH = 24
LANES = 128
XPOS = 32
COEFS = 8
RIM = COEFS * (DEPTH - 1) * SIDE + DEPTH * SIDE
CORNER = 120
F32 = jnp.float32
BF16 = jnp.bfloat16


def box_grid(box_count):
    box_rows = max(2, min(8, box_count // 4))
    return box_rows, box_count // box_rows


def split(value):
    high = value.astype(BF16)
    return high, (value - high.astype(F32)).astype(BF16)


def cell_planes(start, count, flag, vol, ap, cond, src, prev, put):
    rows = pl.ds(start, count)
    regular = flag == 1
    covered = flag == 0
    inverse = 1.0 / cond[rows, :].astype(F32)
    fraction = jnp.where(regular, 1.0, vol[rows, :].astype(F32))
    for face in range(6):
        value = ap[face, rows, :].astype(F32)
        put(face, slice(None), jnp.where(regular, 1.0, jnp.where(covered, 0.0, value)))
    put(6, slice(None), jnp.where(covered, 1.0, (SIGMA * fraction) * inverse))
    scale = fraction * inverse
    for half in range(2):
        cells = slice(half * LANES, (half + 1) * LANES)
        picked = pl.ds(2 * start + half, count, stride=2)
        before = prev[picked, :]
        put(7, cells, jnp.where(covered, before, scale[:, cells] * src[picked, :]))
        put(8, cells, before)


def pack_kernel(*refs):
    sources, (send_a, send_b), copies, semaphores = refs[:7], refs[7:9], refs[9:16], refs[16]
    moves = [
        pltpu.make_async_copy(source, copy, semaphores.at[index])
        for index, (source, copy) in enumerate(zip(sources, copies, strict=True))
    ]
    for move in moves:
        move.start()
    vol, ap, cond, src, prev, flags, _ = copies
    group = lax.axis_index("grp")
    column = lax.axis_index("box")
    for move in moves:
        move.wait()

    def emit(out, first):
        for layer in range(LPD):
            low, high = max(layer * SIDE, first), min((layer + 1) * SIDE, first + REACH)
            if low >= high:
                continue
            rows = pl.ds(low - first, high - low)

            def put(plane, cells, value, rows=rows):
                if plane == 7:
                    out[7, rows, cells], out[9, rows, cells] = split(value)
                else:
                    out[plane, rows, cells] = value.astype(BF16)

            cell_planes(low, high - low, flags[column, group * LPD + layer], vol, ap, cond, src, prev, put)

    for odd in (0, 1):

        @pl.when(group % 2 == odd)
        def _():
            emit(send_a, 0 if odd else ROWS - REACH)
            emit(send_b, ROWS - REACH if odd else 0)


def own_kernel(vol, ap, cond, src, prev, flags, own):
    group = lax.axis_index("grp")
    column = lax.axis_index("box")
    for layer in range(LPD):

        def put(plane, cells, value, rows=pl.ds(layer * SIDE, SIDE)):
            own[plane, rows, cells] = value

        cell_planes(layer * SIDE, SIDE, flags[column, group * LPD + layer], vol, ap, cond, src, prev, put)


def corner_runs():
    runs = []
    row = 0
    for plane in range(COEFS + 1):
        reach = DEPTH - 1 if plane < COEFS else DEPTH
        for dy in range(1, DEPTH):
            run = reach - (dy + 1) // 2 * 2 + 1
            if run > 0:
                runs.append((plane, dy, run, row))
                row += run
    return runs


def turn_kernel(box_rows, box_cols, own, from_a, from_b, turned, *refs):
    rims, stage = refs[:-1], refs[-1]
    even_group = lax.axis_index("grp") % 2 == 0
    box_y = lax.axis_index("box") // box_cols
    used = REACH + ROWS + REACH
    stage[pl.ds(used, LANES - used), :] = jnp.zeros((LANES - used, CELLS), F32)
    for plane in range(9):
        a = from_a[plane, :, :].astype(F32)
        b = from_b[plane, :, :].astype(F32)
        if plane == 7:
            a = a + from_a[9, :, :].astype(F32)
            b = b + from_b[9, :, :].astype(F32)
        stage[pl.ds(0, REACH), :] = jnp.where(even_group, b, a)
        stage[pl.ds(REACH, ROWS), :] = own[plane, :, :]
        stage[pl.ds(REACH + ROWS, REACH), :] = jnp.where(even_group, a, b)
        for half in range(2):
            turned[plane, pl.ds(half * LANES, LANES), :] = stage[:, pl.ds(half * LANES, LANES)].T

    def rim(out, high):
        for plane in range(COEFS + 1):
            reach = DEPTH - 1 if plane < COEFS else DEPTH
            start = (SIDE - reach) * SIDE if high else 0
            out[pl.ds(plane * (DEPTH - 1) * SIDE, reach * SIDE), :] = turned[
                plane, pl.ds(start, reach * SIDE), :
            ].astype(BF16)

    for odd in (0, 1):

        @pl.when(box_y % 2 == odd)
        def _():
            for kind, out in enumerate(rims):
                rim(out, odd == kind)


def rims_kernel(box_rows, box_cols, turned, *refs):
    rims, corners, stage = refs[:2], refs[2:-1], refs[-1]
    box_x = lax.axis_index("box") % box_cols
    box_y = lax.axis_index("box") // box_cols

    def rim(out, high):
        for plane in range(COEFS + 1):
            reach = DEPTH - 1 if plane < COEFS else DEPTH
            for i in range(reach):
                x = SIDE - reach + i if high else i
                pair = [turned[plane, pl.ds(x + odd * SIDE, SIDE // 2, stride=2 * SIDE), :] for odd in (0, 1)]
                out[pl.ds((plane * (DEPTH - 1) + i) * SIDE, SIDE), :] = jnp.concatenate(pair, axis=0).astype(BF16)

    def corner(out, high_y, high_x):
        for plane, dy, run, row in corner_runs():
            y = SIDE - dy if high_y else dy - 1
            x = SIDE - run if high_x else 0
            stage[pl.ds(row, run), :] = turned[plane, pl.ds(y * SIDE + x, run), :]
        used = corner_runs()[-1][2] + corner_runs()[-1][3]
        stage[pl.ds(used, CORNER - used), :] = jnp.zeros((CORNER - used, LANES), F32)
        out[...] = stage[...].astype(BF16)

    for odd_x in (0, 1):

        @pl.when(box_x % 2 == odd_x)
        def _():
            rim(rims[0], odd_x == 0)
            rim(rims[1], odd_x == 1)

        for odd_y in (0, 1):

            @pl.when((box_y % 2 == odd_y) & (box_x % 2 == odd_x))
            def _():
                for index, out in enumerate(corners):
                    corner(out, odd_y == index // 2, odd_x == index % 2)


def normal(values):
    total = values[6]
    for face in range(6):
        total = total + values[face]
    inverse = 1.0 / jnp.where(total > 0.0, total, 1.0)
    return [values[face] * inverse for face in range(6)] + [values[7] * inverse]


def rows_of(box_rows):
    return SIDE + DEPTH * (1 if box_rows == 2 else 2)


def pairs_of(box_rows):
    return rows_of(box_rows) // 2


def odd_cells(count, first_x):
    shape = (count, LANES)
    cells = lax.broadcasted_iota(jnp.int32, shape, 0) + lax.broadcasted_iota(jnp.int32, shape, 1)
    return (cells + first_x) % 2 == 1


def odd_lanes(count, x):
    return (lax.broadcasted_iota(jnp.int32, (count, LANES), 1) + x) % 2 == 1


def put_pair(grid, plane, rows, odd, low, high):
    planes, *states = grid
    red, black = jnp.where(odd, high, low), jnp.where(odd, low, high)
    if plane == COEFS - 1:
        states[0][rows, :] = red
        states[1][rows, :] = black
    else:
        planes[0, plane, rows, :] = red
        planes[1, plane, rows, :] = black


def slab(rim, index):
    return rim[pl.ds(index * SIDE, SIDE), :].astype(F32)


def prepare_kernel(box_rows, box_cols, turned, *grid):
    box_y = lax.axis_index("box") // box_cols
    low_open = jnp.where(box_y > 0, 1.0, 0.0).astype(F32)
    high_open = jnp.where(box_y < box_rows - 1, 1.0, 0.0).astype(F32)
    odd = odd_cells(SIDE, 0)

    def weights_at(y):
        weights = normal([turned[plane, pl.ds(y * SIDE, SIDE), :] for plane in range(COEFS)])
        if y == 0:
            weights[2] = weights[2] * low_open
        if y == SIDE - 1:
            weights[3] = weights[3] * high_open
        return weights + [turned[8, pl.ds(y * SIDE, SIDE), :]]

    for k in range(pairs_of(box_rows)):
        own = 2 * k < SIDE
        clear = pl.ds(k * XPOS + SIDE, SIDE) if own else pl.ds(k * XPOS, XPOS)
        empty = jnp.zeros((SIDE if own else XPOS, LANES), F32)
        for plane in range(COEFS):
            put_pair(grid, plane, clear, empty > 0.0, empty, empty)
        if own:
            for plane, (low, high) in enumerate(zip(weights_at(2 * k), weights_at(2 * k + 1), strict=True)):
                put_pair(grid, plane, pl.ds(k * XPOS, SIDE), odd, low, high)


def sides_kernel(box_rows, box_cols, *refs):
    rims, grid = refs[3:-3], refs[-3:]
    box_x = lax.axis_index("box") % box_cols
    box_y = lax.axis_index("box") // box_cols
    low_pair = pairs_of(box_rows) - DEPTH // 2
    high_pair = SIDE // 2

    def place_y(rim, high):
        odd = odd_cells(SIDE, 0)
        empty = jnp.zeros((SIDE, LANES), F32)

        def weights_at(i):
            i = i if high else i - 1
            if not 0 <= i < DEPTH - 1:
                return [empty] * (COEFS - 1)
            return normal([slab(rim, plane * (DEPTH - 1) + i) for plane in range(COEFS)])

        for j in range(DEPTH // 2):
            rows = pl.ds(((high_pair if high else low_pair) + j) * XPOS, SIDE)
            two = [weights_at(2 * j + i) + [slab(rim, COEFS * (DEPTH - 1) + 2 * j + i)] for i in (0, 1)]
            for plane, (low_value, high_value) in enumerate(zip(*two, strict=True)):
                put_pair(grid, plane, rows, odd, low_value, high_value)

    def place_x(rim, high):
        half = SIDE // 2
        for i in range(DEPTH):
            x = SIDE + i if high else XPOS - DEPTH + i
            at = i if high else i - 1
            rows = pl.ds(x, half, stride=XPOS)
            odd = odd_lanes(half, x)
            if 0 <= at < DEPTH - 1:
                for plane, value in enumerate(normal([slab(rim, plane * (DEPTH - 1) + at) for plane in range(COEFS)])):
                    put_pair(grid, plane, rows, odd, value[:half], value[half:])
            value = slab(rim, COEFS * (DEPTH - 1) + i)
            put_pair(grid, 7, rows, odd, value[:half], value[half:])

    for odd_x in (0, 1):

        @pl.when(box_x % 2 == odd_x)
        def _():
            place_x(rims[-2], odd_x == 0)
            place_x(rims[-1], odd_x == 1)

    for odd_y in (0, 1):

        @pl.when(box_y % 2 == odd_y)
        def _():
            for kind, rim in enumerate(rims[:-2]):
                place_y(rim, odd_y == kind)


def smooth_kernel(box_rows, box_cols, kinds, *refs):
    refs = refs[3:]
    pieces = dict(zip(kinds, refs[: len(kinds)], strict=True))
    groups, out, planes, *states, result = refs[len(kinds) :]
    grid = (planes, *states)
    pair_count = pairs_of(box_rows)
    low_pair = pair_count - DEPTH // 2
    high_pair = SIDE // 2
    group = lax.axis_index("grp")
    box_x = lax.axis_index("box") % box_cols
    box_y = lax.axis_index("box") // box_cols

    def place_corner(piece, high_y, high_x):
        cells = piece[...].astype(F32)
        found = {(plane, dy): cells[row : row + run, :] for plane, dy, run, row in corner_runs()}
        for j in range(DEPTH // 2):
            k = (high_pair + j if high_y else low_pair + DEPTH // 2 - 1 - j) * XPOS
            near = [2 * j + 1, 2 * j + 2] if high_y else [2 * j + 2, 2 * j + 1]
            groups_of = []
            if (0, near[0]) in found:
                two = [normal([found[plane, dy] for plane in range(COEFS)]) for dy in near]
                groups_of += [(plane, low, high) for plane, (low, high) in enumerate(zip(*two, strict=True))]
            if (COEFS, 2 * j + 1) in found:
                pair = [found.get((COEFS, dy), jnp.zeros_like(found[COEFS, 2 * j + 1])) for dy in near]
                groups_of.append((7, *pair))
            for plane, low, high in groups_of:
                run = low.shape[0]
                x = SIDE if high_x else XPOS - run
                put_pair(grid, plane, pl.ds(k + x, run), odd_cells(run, x), low, high)

    for odd_y in (0, 1):
        for odd_x in (0, 1):

            @pl.when((box_y % 2 == odd_y) & (box_x % 2 == odd_x))
            def _():
                for (kind_y, kind_x), piece in pieces.items():
                    if None not in (kind_y, kind_x):
                        place_corner(piece, odd_y == kind_y, odd_x == kind_x)

    odd = odd_cells(XPOS, 0)

    def update(colour, k):
        def at(offset):
            if isinstance(k, int):
                return pl.ds((k + offset) % pair_count * XPOS, XPOS)
            return pl.ds(pl.multiple_of(lax.rem(k + (offset + pair_count), pair_count) * XPOS, XPOS), XPOS)

        here = states[1 - colour][at(0), :]
        below = states[1 - colour][at(-1), :]
        above = states[1 - colour][at(1), :]
        if colour == 0:
            low, high = jnp.where(odd, here, below), jnp.where(odd, above, here)
        else:
            low, high = jnp.where(odd, below, here), jnp.where(odd, here, above)
        adjacent = (
            pltpu.roll(here, 1, 1),
            pltpu.roll(here, LANES - 1, 1),
            low,
            high,
            pltpu.roll(here, 1, 0),
            pltpu.roll(here, XPOS - 1, 0),
        )
        gathered = planes[colour, 6, at(0), :]
        for face in range(6):
            gathered = gathered + planes[colour, face, at(0), :] * adjacent[face]
        states[colour][at(0), :] = gathered

    even_row = box_y % 2 == 0
    for half_sweep in range(2 * SWEEPS):
        colour = half_sweep % 2
        for k in range(high_pair):
            update(colour, k)
        for j in range((DEPTH - half_sweep) // 2):
            if box_rows == 2:
                update(colour, jnp.where(even_row, high_pair + j, pair_count - 1 - j))
            else:
                update(colour, high_pair + j)
                update(colour, pair_count - 1 - j)

    odd = odd_cells(SIDE, 0)
    for half in range(2):
        cells = []
        for k in range(half * 4, half * 4 + 4):
            red = states[0][pl.ds(k * XPOS, SIDE), :]
            black = states[1][pl.ds(k * XPOS, SIDE), :]
            cells += [jnp.where(odd, black, red), jnp.where(odd, red, black)]
        result[pl.ds(0, LANES), pl.ds(half * LANES, LANES)] = jnp.concatenate(cells, axis=0).T
    count = jnp.int32(0)
    first = jnp.int32(0)
    for layer in range(groups.shape[0]):
        owner = groups[layer]
        count = count + jnp.where(owner == group, 1, 0)
        first = first + jnp.where(owner < group, 1, 0)
    start = pl.multiple_of(REACH + (first - group * LPD) * SIDE, 8)
    valid = lax.broadcasted_iota(jnp.int32, (OUT_ROWS, LANES), 0) < count * SIDE
    for half in range(2):
        value = result[pl.ds(start, OUT_ROWS), pl.ds(half * LANES, LANES)]
        out[pl.ds(half, OUT_ROWS, stride=2), :] = jnp.where(valid, value, 0.0)


def swaps(count, kind):
    pairs = []
    for low in range(kind, count - 1, 2):
        pairs += [(low, low + 1), (low + 1, low)]
    return pairs


def lateral_pairs(box_rows, box_cols, kind_y, kind_x):
    move_y = dict(swaps(box_rows, kind_y)) if kind_y is not None else {i: i for i in range(box_rows)}
    move_x = dict(swaps(box_cols, kind_x)) if kind_x is not None else {i: i for i in range(box_cols)}
    return [
        (y * box_cols + x, move_y[y] * box_cols + move_x[x])
        for y in range(box_rows)
        for x in range(box_cols)
        if y in move_y and x in move_x
    ]


def vmem(count):
    return [pl.BlockSpec(memory_space=pltpu.VMEM)] * count


def held(*arrays):
    return [pltpu.with_memory_space_constraint(array, pltpu.VMEM) for array in arrays]


def params():
    return pltpu.CompilerParams(vmem_limit_bytes=16 * 2**20)


def per_device(volume, apertures, conductivity, source, previous, cut_flags, new_group):
    group_count = lax.axis_size("grp")
    box_rows, box_cols = box_grid(lax.axis_size("box"))
    smem = pl.BlockSpec(memory_space=pltpu.SMEM)
    raw = (
        volume.reshape(ROWS, CELLS),
        apertures.reshape(6, ROWS, CELLS),
        conductivity.reshape(ROWS, CELLS),
        source.reshape(2 * ROWS, LANES),
        previous.reshape(2 * ROWS, LANES),
        cut_flags.T,
        new_group,
    )
    send_a, send_b, *local = pl.pallas_call(
        pack_kernel,
        out_shape=[pltpu.VMEM((10, REACH, CELLS), BF16)] * 2
        + [pltpu.VMEM(array.shape, array.dtype) for array in raw[:5]]
        + [pltpu.SMEM(array.shape, array.dtype) for array in raw[5:]],
        in_specs=[pl.BlockSpec(memory_space=pltpu.HBM)] * 7,
        out_specs=vmem(7) + [smem] * 2,
        scratch_shapes=[pltpu.SemaphoreType.DMA((7,))],
        compiler_params=params(),
        name="pack",
    )(*[pltpu.with_memory_space_constraint(array, pltpu.HBM) for array in raw])
    from_a = lax.ppermute(send_a, "grp", swaps(group_count, 0))
    from_b = lax.ppermute(send_b, "grp", swaps(group_count, 1))
    own = pl.pallas_call(
        own_kernel,
        out_shape=pltpu.VMEM((9, ROWS, CELLS), F32),
        in_specs=vmem(5) + [smem],
        out_specs=vmem(1)[0],
        compiler_params=params(),
        cost_estimate=pl.CostEstimate(flops=4 * 2**20, bytes_accessed=2**20, transcendentals=0),
        name="own",
    )(*held(*local[:5]), local[5])

    kinds_y = [0] if box_rows == 2 else [0, 1]
    kinds = [(kind, None) for kind in kinds_y] + [(None, 0), (None, 1)]
    kinds += [(kind_y, kind_x) for kind_y in kinds_y for kind_x in (0, 1)]
    shapes = [pltpu.VMEM((RIM if None in kind else CORNER, LANES), BF16) for kind in kinds]
    turned, *sends = pl.pallas_call(
        lambda *refs: turn_kernel(box_rows, box_cols, *refs),
        out_shape=[pltpu.VMEM((9, CELLS, LANES), F32)] + shapes[: len(kinds_y)],
        in_specs=vmem(3),
        out_specs=vmem(1 + len(kinds_y)),
        scratch_shapes=[pltpu.VMEM((LANES, CELLS), F32)],
        compiler_params=params(),
        name="turn",
    )(*held(own, from_a, from_b))
    sends += pl.pallas_call(
        lambda *refs: rims_kernel(box_rows, box_cols, *refs),
        out_shape=shapes[len(kinds_y) :],
        in_specs=vmem(1),
        out_specs=vmem(len(shapes) - len(kinds_y)),
        scratch_shapes=[pltpu.VMEM((CORNER, LANES), F32)],
        compiler_params=params(),
        cost_estimate=pl.CostEstimate(flops=2**20, bytes_accessed=2**20, transcendentals=0),
        name="rims",
    )(*held(turned))
    arrived = [
        lax.ppermute(send, "box", lateral_pairs(box_rows, box_cols, *kind))
        for send, kind in zip(sends, kinds, strict=True)
    ]
    sides = [array for array, kind in zip(arrived, kinds, strict=True) if None in kind]
    arrived = [array for array, kind in zip(arrived, kinds, strict=True) if None not in kind]
    kinds = [kind for kind in kinds if None not in kind]
    cells = pairs_of(box_rows) * XPOS
    grid_shapes = [pltpu.VMEM((2, COEFS - 1, cells, LANES), F32)] + [pltpu.VMEM((cells, LANES), F32)] * 2
    grid = pl.pallas_call(
        lambda *refs: prepare_kernel(box_rows, box_cols, *refs),
        out_shape=grid_shapes,
        in_specs=vmem(1),
        out_specs=vmem(3),
        compiler_params=params(),
        cost_estimate=pl.CostEstimate(flops=8 * 2**20, bytes_accessed=2**20, transcendentals=0),
        name="prepare",
    )(*held(turned))
    grid = pl.pallas_call(
        lambda *refs: sides_kernel(box_rows, box_cols, *refs),
        out_shape=grid_shapes,
        in_specs=vmem(3 + len(sides)),
        out_specs=vmem(3),
        input_output_aliases={0: 0, 1: 1, 2: 2},
        compiler_params=params(),
        cost_estimate=pl.CostEstimate(flops=2**10, bytes_accessed=2**10, transcendentals=0),
        name="sides",
    )(*held(*grid, *sides))
    smoothed, *_ = pl.pallas_call(
        lambda *refs: smooth_kernel(box_rows, box_cols, kinds, *refs),
        out_shape=[jax.ShapeDtypeStruct((2 * OUT_ROWS, LANES), F32)] + grid_shapes,
        in_specs=vmem(3 + len(kinds)) + [smem],
        out_specs=vmem(4),
        scratch_shapes=[pltpu.VMEM((REACH + SIDE + OUT_ROWS, CELLS), F32)],
        input_output_aliases={0: 1, 1: 2, 2: 3},
        compiler_params=params(),
        name="smooth",
    )(*held(*grid, *arrived), local[6])
    return smoothed.reshape(OUT_ROWS, 1, CELLS)


def solution(mesh):
    in_specs = (
        P("grp", "box", None),
        P(None, "grp", "box", None),
        P("grp", "box", None),
        P("grp", "box", None),
        P("grp", "box", None),
        P(),
        P(),
    )
    out_specs = P("grp", "box", None)
    return jax.shard_map(
        per_device, mesh=mesh, in_specs=in_specs, out_specs=out_specs, check_vma=False
    )
```

```python
import jax
import jax.numpy as jnp
from jax import lax
from jax.experimental import pallas as pl
from jax.experimental.pallas import tpu as pltpu
from jax.sharding import PartitionSpec as P

SIDE = 16
LPD = 4
SWEEPS = 3
SIGMA = 0.05
CELLS = SIDE * SIDE
ROWS = LPD * SIDE
OUT_ROWS = (LPD + 2) * SIDE
DEPTH = 2 * SWEEPS
REACH = 24
LANES = 128
XPOS = 32
COEFS = 8
CORNER = 120
NEAR = DEPTH - 2
USED = REACH + ROWS + REACH
SPARE = LANES - USED
RIM_SLABS = COEFS * NEAR + COEFS // 2 + DEPTH
RIM = RIM_SLABS * SIDE
F32 = jnp.float32
BF16 = jnp.bfloat16


def box_grid(box_count):
    box_rows = max(2, min(8, box_count // 4))
    return box_rows, box_count // box_rows


def split(value):
    high = value.astype(BF16)
    return high, (value - high.astype(F32)).astype(BF16)


def cell_planes(start, count, flag, vol, ap, cond, src, prev, put):
    rows = pl.ds(start, count)
    regular = flag == 1
    covered = flag == 0
    inverse = 1.0 / cond[rows, :].astype(F32)
    fraction = jnp.where(regular, 1.0, vol[rows, :].astype(F32))
    for face in range(6):
        value = ap[face, rows, :].astype(F32)
        put(face, slice(None), jnp.where(regular, 1.0, jnp.where(covered, 0.0, value)))
    put(6, slice(None), jnp.where(covered, 1.0, (SIGMA * fraction) * inverse))
    scale = fraction * inverse
    for half in range(2):
        cells = slice(half * LANES, (half + 1) * LANES)
        picked = pl.ds(2 * start + half, count, stride=2)
        before = prev[picked, :]
        put(7, cells, jnp.where(covered, before, scale[:, cells] * src[picked, :]))
        put(8, cells, before)


def pack_kernel(*refs):
    sources, (send_a, send_b), copies, semaphores = refs[:7], refs[7:9], refs[9:16], refs[16]
    moves = [
        pltpu.make_async_copy(source, copy, semaphores.at[index])
        for index, (source, copy) in enumerate(zip(sources, copies, strict=True))
    ]
    for move in moves:
        move.start()
    vol, ap, cond, src, prev, flags, _ = copies
    group = lax.axis_index("grp")
    column = lax.axis_index("box")
    for move in moves:
        move.wait()

    def emit(out, first):
        for layer in range(LPD):
            low, high = max(layer * SIDE, first), min((layer + 1) * SIDE, first + REACH)
            if low >= high:
                continue
            rows = pl.ds(low - first, high - low)

            def put(plane, cells, value, rows=rows):
                if plane == 7:
                    out[7, rows, cells], out[9, rows, cells] = split(value)
                else:
                    out[plane, rows, cells] = value.astype(BF16)

            cell_planes(low, high - low, flags[column, group * LPD + layer], vol, ap, cond, src, prev, put)

    for odd in (0, 1):

        @pl.when(group % 2 == odd)
        def _():
            emit(send_a, 0 if odd else ROWS - REACH)
            emit(send_b, ROWS - REACH if odd else 0)


def own_kernel(vol, ap, cond, src, prev, flags, own):
    group = lax.axis_index("grp")
    column = lax.axis_index("box")
    for layer in range(LPD):

        def put(plane, cells, value, rows=pl.ds(layer * SIDE, SIDE)):
            own[plane, rows, cells] = value

        cell_planes(layer * SIDE, SIDE, flags[column, group * LPD + layer], vol, ap, cond, src, prev, put)


def corner_runs():
    runs = []
    row = 0
    for plane in range(COEFS + 1):
        reach = DEPTH - 1 if plane < COEFS else DEPTH
        for dy in range(1, DEPTH):
            run = reach - (dy + 1) // 2 * 2 + 1
            if run > 0:
                runs.append((plane, dy, run, row))
                row += run
    return runs


def odd_cells(count, first_x):
    shape = (count, LANES)
    cells = lax.broadcasted_iota(jnp.int32, shape, 0) + lax.broadcasted_iota(jnp.int32, shape, 1)
    return (cells + first_x) % 2 == 1


def odd_lanes(count, x):
    return (lax.broadcasted_iota(jnp.int32, (count, LANES), 1) + x) % 2 == 1


def odd_split(x):
    row = lax.broadcasted_iota(jnp.int32, (SIDE, LANES), 0) // (SIDE // 2)
    return (row + lax.broadcasted_iota(jnp.int32, (SIDE, LANES), 1) + x) % 2 == 1


def write_rim(out, at, high, odd_far):
    values = []
    for i in range(1, DEPTH - 1) if high else range(NEAR):
        values += [at(plane, i) for plane in range(COEFS)]
    far = 0 if high else NEAR
    for plane in range(0, COEFS, 2):
        values.append(jnp.where(odd_far, pltpu.roll(at(plane + 1, far), 1, 1), at(plane, far)))
    for i in range(DEPTH):
        values.append(at(COEFS, i - 1 if high else i))
    for index, value in enumerate(values):
        out[pl.ds(index * SIDE, SIDE), :] = value.astype(BF16)


def slab(rim, index):
    return rim[pl.ds(index * SIDE, SIDE), :].astype(F32)


def read_rim(rim, i, high, odd_far):
    if i == (NEAR if high else 0):
        values = []
        for plane in range(COEFS // 2):
            both = slab(rim, COEFS * NEAR + plane)
            values += [jnp.where(odd_far, 0.0, both), jnp.where(odd_far, 0.0, pltpu.roll(both, LANES - 1, 1))]
        return normal(values)
    start = (i if high else i - 1) * COEFS
    return normal([slab(rim, start + plane) for plane in range(COEFS)])


def turn_kernel(box_rows, box_cols, own, from_a, from_b, turned, *refs):
    rims, stage = refs[:-1], refs[-1]
    even_group = lax.axis_index("grp") % 2 == 0
    box_y = lax.axis_index("box") // box_cols
    stage[pl.ds(USED, SPARE), :] = jnp.zeros((SPARE, CELLS), F32)
    for plane in range(9):
        a = from_a[plane, :, :].astype(F32)
        b = from_b[plane, :, :].astype(F32)
        if plane == 7:
            a = a + from_a[9, :, :].astype(F32)
            b = b + from_b[9, :, :].astype(F32)
        stage[pl.ds(0, REACH), :] = jnp.where(even_group, b, a)
        stage[pl.ds(REACH, ROWS), :] = own[plane, :, :]
        stage[pl.ds(REACH + ROWS, REACH), :] = jnp.where(even_group, a, b)
        for half in range(2):
            turned[plane, pl.ds(half * LANES, LANES), :] = stage[:, pl.ds(half * LANES, LANES)].T

    def rim(out, high):
        first = SIDE - DEPTH + 1 if high else 0

        def at(plane, i):
            return turned[plane, pl.ds((first + i) * SIDE, SIDE), :]

        write_rim(out, at, high, odd_cells(SIDE, first if high else NEAR))

    for odd in (0, 1):

        @pl.when(box_y % 2 == odd)
        def _():
            for kind, out in enumerate(rims):
                rim(out, odd == kind)


def rims_kernel(box_cols, turned, *refs):
    rims = refs[-2:]
    box_x = lax.axis_index("box") % box_cols

    def rim(out, high):
        first = SIDE - DEPTH + 1 if high else 0

        def at(plane, i):
            pair = [
                turned[plane, pl.ds(first + i + odd * SIDE, SIDE // 2, stride=2 * SIDE), :] for odd in (0, 1)
            ]
            return jnp.concatenate(pair, axis=0)

        write_rim(out, at, high, odd_split(first if high else NEAR))

    for odd_x in (0, 1):

        @pl.when(box_x % 2 == odd_x)
        def _():
            rim(rims[0], odd_x == 0)
            rim(rims[1], odd_x == 1)


def corners_kernel(box_cols, turned, *refs):
    corners, stage = refs[:-1], refs[-1]
    box_x = lax.axis_index("box") % box_cols
    box_y = lax.axis_index("box") // box_cols

    def corner(out, high_y, high_x):
        for plane, dy, run, row in corner_runs():
            y = SIDE - dy if high_y else dy - 1
            x = SIDE - run if high_x else 0
            stage[pl.ds(row, run), :] = turned[plane, pl.ds(y * SIDE + x, run), :]
        used = corner_runs()[-1][2] + corner_runs()[-1][3]
        stage[pl.ds(used, CORNER - used), :] = jnp.zeros((CORNER - used, LANES), F32)
        out[...] = stage[...].astype(BF16)

    for odd_x in (0, 1):
        for odd_y in (0, 1):

            @pl.when((box_y % 2 == odd_y) & (box_x % 2 == odd_x))
            def _():
                for index, out in enumerate(corners):
                    corner(out, odd_y == index // 2, odd_x == index % 2)


def normal(values):
    total = values[6]
    for face in range(6):
        total = total + values[face]
    inverse = 1.0 / jnp.where(total > 0.0, total, 1.0)
    return [values[face] * inverse for face in range(6)] + [values[7] * inverse]


def rows_of(box_rows):
    return SIDE + DEPTH * (1 if box_rows == 2 else 2)


def pairs_of(box_rows):
    return rows_of(box_rows) // 2


def put_pair(grid, plane, rows, odd, low, high):
    planes, *states = grid
    red, black = jnp.where(odd, high, low), jnp.where(odd, low, high)
    if plane == COEFS - 1:
        states[0][rows, :] = red
        states[1][rows, :] = black
    else:
        planes[0, plane, rows, :] = red
        planes[1, plane, rows, :] = black


def prepare_kernel(box_rows, box_cols, turned, *grid):
    box_y = lax.axis_index("box") // box_cols
    low_open = jnp.where(box_y > 0, 1.0, 0.0).astype(F32)
    high_open = jnp.where(box_y < box_rows - 1, 1.0, 0.0).astype(F32)
    odd = odd_cells(SIDE, 0)

    def weights_at(y):
        weights = normal([turned[plane, pl.ds(y * SIDE, SIDE), :] for plane in range(COEFS)])
        if y == 0:
            weights[2] = weights[2] * low_open
        if y == SIDE - 1:
            weights[3] = weights[3] * high_open
        return weights + [turned[8, pl.ds(y * SIDE, SIDE), :]]

    for k in range(pairs_of(box_rows)):
        own = 2 * k < SIDE
        clear = pl.ds(k * XPOS + SIDE, SIDE) if own else pl.ds(k * XPOS, XPOS)
        empty = jnp.zeros((SIDE if own else XPOS, LANES), F32)
        for plane in range(COEFS):
            put_pair(grid, plane, clear, empty > 0.0, empty, empty)
        if own:
            for plane, (low, high) in enumerate(zip(weights_at(2 * k), weights_at(2 * k + 1), strict=True)):
                put_pair(grid, plane, pl.ds(k * XPOS, SIDE), odd, low, high)


def sides_kernel(box_rows, box_cols, *refs):
    rims, grid = refs[3:-3], refs[-3:]
    box_x = lax.axis_index("box") % box_cols
    box_y = lax.axis_index("box") // box_cols
    low_pair = pairs_of(box_rows) - DEPTH // 2
    high_pair = SIDE // 2

    def place_y(rim, high):
        odd = odd_cells(SIDE, 0)
        empty = jnp.zeros((SIDE, LANES), F32)

        def weights_at(i):
            at = i if high else i - 1
            if not 0 <= at < DEPTH - 1:
                return [empty] * (COEFS - 1)
            return read_rim(rim, at, high, odd_cells(SIDE, i))

        for j in range(DEPTH // 2):
            rows = pl.ds(((high_pair if high else low_pair) + j) * XPOS, SIDE)
            two = [weights_at(2 * j + i) + [slab(rim, RIM_SLABS - DEPTH + 2 * j + i)] for i in (0, 1)]
            for plane, (low_value, high_value) in enumerate(zip(*two, strict=True)):
                put_pair(grid, plane, rows, odd, low_value, high_value)

    def place_x(rim, high):
        half = SIDE // 2
        for i in range(DEPTH):
            x = SIDE + i if high else XPOS - DEPTH + i
            at = i if high else i - 1
            rows = pl.ds(x, half, stride=XPOS)
            odd = odd_lanes(half, x)
            if 0 <= at < DEPTH - 1:
                for plane, value in enumerate(read_rim(rim, at, high, odd_split(x))):
                    put_pair(grid, plane, rows, odd, value[:half], value[half:])
            value = slab(rim, RIM_SLABS - DEPTH + i)
            put_pair(grid, 7, rows, odd, value[:half], value[half:])

    for odd_x in (0, 1):

        @pl.when(box_x % 2 == odd_x)
        def _():
            place_x(rims[-2], odd_x == 0)
            place_x(rims[-1], odd_x == 1)

    for odd_y in (0, 1):

        @pl.when(box_y % 2 == odd_y)
        def _():
            for kind, rim in enumerate(rims[:-2]):
                place_y(rim, odd_y == kind)


def smooth_kernel(box_rows, box_cols, kinds, *refs):
    refs = refs[3:]
    pieces = dict(zip(kinds, refs[: len(kinds)], strict=True))
    groups, out, planes, *states, result = refs[len(kinds) :]
    grid = (planes, *states)
    pair_count = pairs_of(box_rows)
    low_pair = pair_count - DEPTH // 2
    high_pair = SIDE // 2
    group = lax.axis_index("grp")
    box_x = lax.axis_index("box") % box_cols
    box_y = lax.axis_index("box") // box_cols

    def place_corner(piece, high_y, high_x):
        cells = piece[...].astype(F32)
        found = {(plane, dy): cells[row : row + run, :] for plane, dy, run, row in corner_runs()}
        for j in range(DEPTH // 2):
            k = (high_pair + j if high_y else low_pair + DEPTH // 2 - 1 - j) * XPOS
            near = [2 * j + 1, 2 * j + 2] if high_y else [2 * j + 2, 2 * j + 1]
            groups_of = []
            if (0, near[0]) in found:
                two = [normal([found[plane, dy] for plane in range(COEFS)]) for dy in near]
                groups_of += [(plane, low, high) for plane, (low, high) in enumerate(zip(*two, strict=True))]
            if (COEFS, 2 * j + 1) in found:
                pair = [found.get((COEFS, dy), jnp.zeros_like(found[COEFS, 2 * j + 1])) for dy in near]
                groups_of.append((7, *pair))
            for plane, low, high in groups_of:
                run = low.shape[0]
                x = SIDE if high_x else XPOS - run
                put_pair(grid, plane, pl.ds(k + x, run), odd_cells(run, x), low, high)

    for odd_y in (0, 1):
        for odd_x in (0, 1):

            @pl.when((box_y % 2 == odd_y) & (box_x % 2 == odd_x))
            def _():
                for (kind_y, kind_x), piece in pieces.items():
                    if None not in (kind_y, kind_x):
                        place_corner(piece, odd_y == kind_y, odd_x == kind_x)

    odd = odd_cells(XPOS, 0)

    def update(colour, k):
        def at(offset):
            if isinstance(k, int):
                return pl.ds((k + offset) % pair_count * XPOS, XPOS)
            return pl.ds(pl.multiple_of(lax.rem(k + (offset + pair_count), pair_count) * XPOS, XPOS), XPOS)

        here = states[1 - colour][at(0), :]
        below = states[1 - colour][at(-1), :]
        above = states[1 - colour][at(1), :]
        if colour == 0:
            low, high = jnp.where(odd, here, below), jnp.where(odd, above, here)
        else:
            low, high = jnp.where(odd, below, here), jnp.where(odd, here, above)
        adjacent = (
            pltpu.roll(here, 1, 1),
            pltpu.roll(here, LANES - 1, 1),
            low,
            high,
            pltpu.roll(here, 1, 0),
            pltpu.roll(here, XPOS - 1, 0),
        )
        gathered = planes[colour, 6, at(0), :]
        for face in range(6):
            gathered = gathered + planes[colour, face, at(0), :] * adjacent[face]
        states[colour][at(0), :] = gathered

    even_row = box_y % 2 == 0
    for half_sweep in range(2 * SWEEPS):
        colour = half_sweep % 2
        for k in range(high_pair):
            update(colour, k)
        for j in range((DEPTH - half_sweep) // 2):
            if box_rows == 2:
                update(colour, jnp.where(even_row, high_pair + j, pair_count - 1 - j))
            else:
                update(colour, high_pair + j)
                update(colour, pair_count - 1 - j)

    odd = odd_cells(SIDE, 0)
    for half in range(2):
        cells = []
        for k in range(half * 4, half * 4 + 4):
            red = states[0][pl.ds(k * XPOS, SIDE), :]
            black = states[1][pl.ds(k * XPOS, SIDE), :]
            cells += [jnp.where(odd, black, red), jnp.where(odd, red, black)]
        result[pl.ds(0, LANES), pl.ds(half * LANES, LANES)] = jnp.concatenate(cells, axis=0).T
    count = jnp.int32(0)
    first = jnp.int32(0)
    for layer in range(groups.shape[0]):
        owner = groups[layer]
        count = count + jnp.where(owner == group, 1, 0)
        first = first + jnp.where(owner < group, 1, 0)
    start = pl.multiple_of(REACH + (first - group * LPD) * SIDE, 8)
    valid = lax.broadcasted_iota(jnp.int32, (OUT_ROWS, LANES), 0) < count * SIDE
    for half in range(2):
        value = result[pl.ds(start, OUT_ROWS), pl.ds(half * LANES, LANES)]
        out[pl.ds(half, OUT_ROWS, stride=2), :] = jnp.where(valid, value, 0.0)


def swaps(count, kind):
    pairs = []
    for low in range(kind, count - 1, 2):
        pairs += [(low, low + 1), (low + 1, low)]
    return pairs


def lateral_pairs(box_rows, box_cols, kind_y, kind_x):
    move_y = dict(swaps(box_rows, kind_y)) if kind_y is not None else {i: i for i in range(box_rows)}
    move_x = dict(swaps(box_cols, kind_x)) if kind_x is not None else {i: i for i in range(box_cols)}
    return [
        (y * box_cols + x, move_y[y] * box_cols + move_x[x])
        for y in range(box_rows)
        for x in range(box_cols)
        if y in move_y and x in move_x
    ]


def vmem(count):
    return [pl.BlockSpec(memory_space=pltpu.VMEM)] * count


def held(*arrays):
    return [pltpu.with_memory_space_constraint(array, pltpu.VMEM) for array in arrays]


def params():
    return pltpu.CompilerParams(vmem_limit_bytes=16 * 2**20)


def per_device(volume, apertures, conductivity, source, previous, cut_flags, new_group):
    group_count = lax.axis_size("grp")
    box_rows, box_cols = box_grid(lax.axis_size("box"))
    smem = pl.BlockSpec(memory_space=pltpu.SMEM)
    raw = (
        volume.reshape(ROWS, CELLS),
        apertures.reshape(6, ROWS, CELLS),
        conductivity.reshape(ROWS, CELLS),
        source.reshape(2 * ROWS, LANES),
        previous.reshape(2 * ROWS, LANES),
        cut_flags.T,
        new_group,
    )
    send_a, send_b, *local = pl.pallas_call(
        pack_kernel,
        out_shape=[pltpu.VMEM((10, REACH, CELLS), BF16)] * 2
        + [pltpu.VMEM(array.shape, array.dtype) for array in raw[:5]]
        + [pltpu.SMEM(array.shape, array.dtype) for array in raw[5:]],
        in_specs=[pl.BlockSpec(memory_space=pltpu.HBM)] * 7,
        out_specs=vmem(7) + [smem] * 2,
        scratch_shapes=[pltpu.SemaphoreType.DMA((7,))],
        compiler_params=params(),
        name="pack",
    )(*[pltpu.with_memory_space_constraint(array, pltpu.HBM) for array in raw])
    from_a = lax.ppermute(send_a, "grp", swaps(group_count, 0))
    from_b = lax.ppermute(send_b, "grp", swaps(group_count, 1))
    own = pl.pallas_call(
        own_kernel,
        out_shape=pltpu.VMEM((9, ROWS, CELLS), F32),
        in_specs=vmem(5) + [smem],
        out_specs=vmem(1)[0],
        compiler_params=params(),
        cost_estimate=pl.CostEstimate(flops=4 * 2**20, bytes_accessed=2**20, transcendentals=0),
        name="own",
    )(*held(*local[:5]), local[5])

    kinds_y = [0] if box_rows == 2 else [0, 1]
    kinds = [(kind, None) for kind in kinds_y] + [(None, 0), (None, 1)]
    kinds += [(kind_y, kind_x) for kind_y in kinds_y for kind_x in (0, 1)]
    shapes = [pltpu.VMEM((RIM if None in kind else CORNER, LANES), BF16) for kind in kinds]
    turned, *sends = pl.pallas_call(
        lambda *refs: turn_kernel(box_rows, box_cols, *refs),
        out_shape=[pltpu.VMEM((9, CELLS, LANES), F32)] + shapes[: len(kinds_y)],
        in_specs=vmem(3),
        out_specs=vmem(1 + len(kinds_y)),
        scratch_shapes=[pltpu.VMEM((LANES, CELLS), F32)],
        compiler_params=params(),
        name="turn",
    )(*held(own, from_a, from_b))
    corners = pl.pallas_call(
        lambda *refs: corners_kernel(box_cols, *refs),
        out_shape=shapes[len(kinds_y) + 2 :],
        in_specs=vmem(1),
        out_specs=vmem(2 * len(kinds_y)),
        scratch_shapes=[pltpu.VMEM((CORNER, LANES), F32)],
        compiler_params=params(),
        cost_estimate=pl.CostEstimate(flops=2**10, bytes_accessed=2**10, transcendentals=0),
        name="corners",
    )(*held(turned))
    sends += pl.pallas_call(
        lambda *refs: rims_kernel(box_cols, *refs),
        out_shape=shapes[len(kinds_y) : len(kinds_y) + 2],
        in_specs=vmem(2),
        out_specs=vmem(2),
        compiler_params=params(),
        cost_estimate=pl.CostEstimate(flops=2**20, bytes_accessed=2**20, transcendentals=0),
        name="rims",
    )(*held(turned, corners[0]))
    sends += corners
    arrived = [
        lax.ppermute(send, "box", lateral_pairs(box_rows, box_cols, *kind))
        for send, kind in zip(sends, kinds, strict=True)
    ]
    sides = [array for array, kind in zip(arrived, kinds, strict=True) if None in kind]
    arrived = [array for array, kind in zip(arrived, kinds, strict=True) if None not in kind]
    kinds = [kind for kind in kinds if None not in kind]
    cells = pairs_of(box_rows) * XPOS
    grid_shapes = [pltpu.VMEM((2, COEFS - 1, cells, LANES), F32)] + [pltpu.VMEM((cells, LANES), F32)] * 2
    grid = pl.pallas_call(
        lambda *refs: prepare_kernel(box_rows, box_cols, *refs),
        out_shape=grid_shapes,
        in_specs=vmem(1),
        out_specs=vmem(3),
        compiler_params=params(),
        cost_estimate=pl.CostEstimate(flops=8 * 2**20, bytes_accessed=2**20, transcendentals=0),
        name="prepare",
    )(*held(turned))
    grid = pl.pallas_call(
        lambda *refs: sides_kernel(box_rows, box_cols, *refs),
        out_shape=grid_shapes,
        in_specs=vmem(3 + len(sides)),
        out_specs=vmem(3),
        input_output_aliases={0: 0, 1: 1, 2: 2},
        compiler_params=params(),
        cost_estimate=pl.CostEstimate(flops=2**10, bytes_accessed=2**10, transcendentals=0),
        name="sides",
    )(*held(*grid, *sides))
    smoothed, *_ = pl.pallas_call(
        lambda *refs: smooth_kernel(box_rows, box_cols, kinds, *refs),
        out_shape=[jax.ShapeDtypeStruct((2 * OUT_ROWS, LANES), F32)] + grid_shapes,
        in_specs=vmem(3 + len(kinds)) + [smem],
        out_specs=vmem(4),
        scratch_shapes=[pltpu.VMEM((REACH + SIDE + OUT_ROWS, CELLS), F32)],
        input_output_aliases={0: 1, 1: 2, 2: 3},
        compiler_params=params(),
        name="smooth",
    )(*held(*grid, *arrived), local[6])
    return smoothed.reshape(OUT_ROWS, 1, CELLS)


def solution(mesh):
    in_specs = (
        P("grp", "box", None),
        P(None, "grp", "box", None),
        P("grp", "box", None),
        P("grp", "box", None),
        P("grp", "box", None),
        P(),
        P(),
    )
    out_specs = P("grp", "box", None)
    return jax.shard_map(
        per_device, mesh=mesh, in_specs=in_specs, out_specs=out_specs, check_vma=False
    )
```

```python
import jax
import jax.numpy as jnp
from jax import lax
from jax.experimental import pallas as pl
from jax.experimental.pallas import tpu as pltpu
from jax.sharding import PartitionSpec as P

SIDE = 16
LPD = 4
SWEEPS = 3
SIGMA = 0.05
CELLS = SIDE * SIDE
ROWS = LPD * SIDE
OUT_ROWS = (LPD + 2) * SIDE
DEPTH = 2 * SWEEPS
REACH = 24
LANES = 128
XPOS = 32
COEFS = 8
RIM = COEFS * (DEPTH - 1) * SIDE + DEPTH * SIDE
CORNER = 120
F32 = jnp.float32
BF16 = jnp.bfloat16


def box_grid(box_count):
    box_rows = max(2, min(8, box_count // 4))
    return box_rows, box_count // box_rows


def split(value):
    high = value.astype(BF16)
    return high, (value - high.astype(F32)).astype(BF16)


def cell_planes(start, count, flag, vol, ap, cond, src, prev, put):
    rows = pl.ds(start, count)
    regular = flag == 1
    covered = flag == 0
    inverse = 1.0 / cond[rows, :].astype(F32)
    fraction = jnp.where(regular, 1.0, vol[rows, :].astype(F32))
    for face in range(6):
        value = ap[face, rows, :].astype(F32)
        put(face, slice(None), jnp.where(regular, 1.0, jnp.where(covered, 0.0, value)))
    put(6, slice(None), jnp.where(covered, 1.0, (SIGMA * fraction) * inverse))
    scale = fraction * inverse
    for half in range(2):
        cells = slice(half * LANES, (half + 1) * LANES)
        picked = pl.ds(2 * start + half, count, stride=2)
        before = prev[picked, :]
        put(7, cells, jnp.where(covered, before, scale[:, cells] * src[picked, :]))
        put(8, cells, before)


def pack_kernel(*refs):
    sources, (send_a, send_b), copies, semaphores = refs[:7], refs[7:9], refs[9:16], refs[16]
    moves = [
        pltpu.make_async_copy(source, copy, semaphores.at[index])
        for index, (source, copy) in enumerate(zip(sources, copies, strict=True))
    ]
    for move in moves:
        move.start()
    vol, ap, cond, src, prev, flags, _ = copies
    group = lax.axis_index("grp")
    column = lax.axis_index("box")
    for move in moves:
        move.wait()

    def emit(out, first):
        for layer in range(LPD):
            low, high = max(layer * SIDE, first), min((layer + 1) * SIDE, first + REACH)
            if low >= high:
                continue
            rows = pl.ds(low - first, high - low)

            def put(plane, cells, value, rows=rows):
                if plane == 7:
                    out[7, rows, cells], out[9, rows, cells] = split(value)
                else:
                    out[plane, rows, cells] = value.astype(BF16)

            cell_planes(low, high - low, flags[column, group * LPD + layer], vol, ap, cond, src, prev, put)

    for odd in (0, 1):

        @pl.when(group % 2 == odd)
        def _():
            emit(send_a, 0 if odd else ROWS - REACH)
            emit(send_b, ROWS - REACH if odd else 0)


def own_kernel(vol, ap, cond, src, prev, flags, own):
    group = lax.axis_index("grp")
    column = lax.axis_index("box")
    for layer in range(LPD):

        def put(plane, cells, value, rows=pl.ds(layer * SIDE, SIDE)):
            own[plane, rows, cells] = value

        cell_planes(layer * SIDE, SIDE, flags[column, group * LPD + layer], vol, ap, cond, src, prev, put)


def corner_runs():
    runs = []
    row = 0
    for plane in range(COEFS + 1):
        reach = DEPTH - 1 if plane < COEFS else DEPTH
        for dy in range(1, DEPTH):
            run = reach - (dy + 1) // 2 * 2 + 1
            if run > 0:
                runs.append((plane, dy, run, row))
                row += run
    return runs


def turn_kernel(box_rows, box_cols, own, from_a, from_b, turned, *refs):
    rims, stage = refs[:-1], refs[-1]
    even_group = lax.axis_index("grp") % 2 == 0
    box_y = lax.axis_index("box") // box_cols
    used = REACH + ROWS + REACH
    stage[pl.ds(used, LANES - used), :] = jnp.zeros((LANES - used, CELLS), F32)
    for plane in range(9):
        a = from_a[plane, :, :].astype(F32)
        b = from_b[plane, :, :].astype(F32)
        if plane == 7:
            a = a + from_a[9, :, :].astype(F32)
            b = b + from_b[9, :, :].astype(F32)
        stage[pl.ds(0, REACH), :] = jnp.where(even_group, b, a)
        stage[pl.ds(REACH, ROWS), :] = own[plane, :, :]
        stage[pl.ds(REACH + ROWS, REACH), :] = jnp.where(even_group, a, b)
        for half in range(2):
            turned[plane, pl.ds(half * LANES, LANES), :] = stage[:, pl.ds(half * LANES, LANES)].T

    def rim(out, high):
        for plane in range(COEFS + 1):
            reach = DEPTH - 1 if plane < COEFS else DEPTH
            start = (SIDE - reach) * SIDE if high else 0
            out[pl.ds(plane * (DEPTH - 1) * SIDE, reach * SIDE), :] = turned[
                plane, pl.ds(start, reach * SIDE), :
            ].astype(BF16)

    for odd in (0, 1):

        @pl.when(box_y % 2 == odd)
        def _():
            for kind, out in enumerate(rims):
                rim(out, odd == kind)


def rims_kernel(box_rows, box_cols, turned, *refs):
    rims, corners, stage = refs[:2], refs[2:-1], refs[-1]
    box_x = lax.axis_index("box") % box_cols
    box_y = lax.axis_index("box") // box_cols

    def rim(out, high):
        for plane in range(COEFS + 1):
            reach = DEPTH - 1 if plane < COEFS else DEPTH
            for i in range(reach):
                x = SIDE - reach + i if high else i
                pair = [turned[plane, pl.ds(x + odd * SIDE, SIDE // 2, stride=2 * SIDE), :] for odd in (0, 1)]
                out[pl.ds((plane * (DEPTH - 1) + i) * SIDE, SIDE), :] = jnp.concatenate(pair, axis=0).astype(BF16)

    def corner(out, high_y, high_x):
        for plane, dy, run, row in corner_runs():
            y = SIDE - dy if high_y else dy - 1
            x = SIDE - run if high_x else 0
            stage[pl.ds(row, run), :] = turned[plane, pl.ds(y * SIDE + x, run), :]
        used = corner_runs()[-1][2] + corner_runs()[-1][3]
        stage[pl.ds(used, CORNER - used), :] = jnp.zeros((CORNER - used, LANES), F32)
        out[...] = stage[...].astype(BF16)

    for odd_x in (0, 1):

        @pl.when(box_x % 2 == odd_x)
        def _():
            rim(rims[0], odd_x == 0)
            rim(rims[1], odd_x == 1)

        for odd_y in (0, 1):

            @pl.when((box_y % 2 == odd_y) & (box_x % 2 == odd_x))
            def _():
                for index, out in enumerate(corners):
                    corner(out, odd_y == index // 2, odd_x == index % 2)


def normal(values):
    total = values[6]
    for face in range(6):
        total = total + values[face]
    inverse = 1.0 / jnp.where(total > 0.0, total, 1.0)
    return [values[face] * inverse for face in range(6)] + [values[7] * inverse]


def rows_of(box_rows):
    return SIDE + DEPTH * (1 if box_rows == 2 else 2)


def pairs_of(box_rows):
    return rows_of(box_rows) // 2


def odd_cells(count, first_x):
    shape = (count, LANES)
    cells = lax.broadcasted_iota(jnp.int32, shape, 0) + lax.broadcasted_iota(jnp.int32, shape, 1)
    return (cells + first_x) % 2 == 1


def odd_lanes(count, x):
    return (lax.broadcasted_iota(jnp.int32, (count, LANES), 1) + x) % 2 == 1


def put_pair(grid, plane, rows, odd, low, high):
    planes, *states = grid
    red, black = jnp.where(odd, high, low), jnp.where(odd, low, high)
    if plane == COEFS - 1:
        states[0][rows, :] = red
        states[1][rows, :] = black
    else:
        planes[0, plane, rows, :] = red
        planes[1, plane, rows, :] = black


def slab(rim, index):
    return rim[pl.ds(index * SIDE, SIDE), :].astype(F32)


def prepare_kernel(box_rows, box_cols, turned, *grid):
    box_y = lax.axis_index("box") // box_cols
    low_open = jnp.where(box_y > 0, 1.0, 0.0).astype(F32)
    high_open = jnp.where(box_y < box_rows - 1, 1.0, 0.0).astype(F32)
    odd = odd_cells(SIDE, 0)

    def weights_at(y):
        weights = normal([turned[plane, pl.ds(y * SIDE, SIDE), :] for plane in range(COEFS)])
        if y == 0:
            weights[2] = weights[2] * low_open
        if y == SIDE - 1:
            weights[3] = weights[3] * high_open
        return weights + [turned[8, pl.ds(y * SIDE, SIDE), :]]

    for k in range(pairs_of(box_rows)):
        own = 2 * k < SIDE
        clear = pl.ds(k * XPOS + SIDE, SIDE) if own else pl.ds(k * XPOS, XPOS)
        empty = jnp.zeros((SIDE if own else XPOS, LANES), F32)
        for plane in range(COEFS):
            put_pair(grid, plane, clear, empty > 0.0, empty, empty)
        if own:
            for plane, (low, high) in enumerate(zip(weights_at(2 * k), weights_at(2 * k + 1), strict=True)):
                put_pair(grid, plane, pl.ds(k * XPOS, SIDE), odd, low, high)


def sides_kernel(box_rows, box_cols, *refs):
    rims, grid = refs[3:-3], refs[-3:]
    box_x = lax.axis_index("box") % box_cols
    box_y = lax.axis_index("box") // box_cols
    low_pair = pairs_of(box_rows) - DEPTH // 2
    high_pair = SIDE // 2

    def place_y(rim, high):
        odd = odd_cells(SIDE, 0)
        empty = jnp.zeros((SIDE, LANES), F32)

        def weights_at(i):
            i = i if high else i - 1
            if not 0 <= i < DEPTH - 1:
                return [empty] * (COEFS - 1)
            return normal([slab(rim, plane * (DEPTH - 1) + i) for plane in range(COEFS)])

        for j in range(DEPTH // 2):
            rows = pl.ds(((high_pair if high else low_pair) + j) * XPOS, SIDE)
            two = [weights_at(2 * j + i) + [slab(rim, COEFS * (DEPTH - 1) + 2 * j + i)] for i in (0, 1)]
            for plane, (low_value, high_value) in enumerate(zip(*two, strict=True)):
                put_pair(grid, plane, rows, odd, low_value, high_value)

    def place_x(rim, high):
        half = SIDE // 2
        for i in range(DEPTH):
            x = SIDE + i if high else XPOS - DEPTH + i
            at = i if high else i - 1
            rows = pl.ds(x, half, stride=XPOS)
            odd = odd_lanes(half, x)
            if 0 <= at < DEPTH - 1:
                for plane, value in enumerate(normal([slab(rim, plane * (DEPTH - 1) + at) for plane in range(COEFS)])):
                    put_pair(grid, plane, rows, odd, value[:half], value[half:])
            value = slab(rim, COEFS * (DEPTH - 1) + i)
            put_pair(grid, 7, rows, odd, value[:half], value[half:])

    for odd_x in (0, 1):

        @pl.when(box_x % 2 == odd_x)
        def _():
            place_x(rims[-2], odd_x == 0)
            place_x(rims[-1], odd_x == 1)

    for odd_y in (0, 1):

        @pl.when(box_y % 2 == odd_y)
        def _():
            for kind, rim in enumerate(rims[:-2]):
                place_y(rim, odd_y == kind)


def smooth_kernel(box_rows, box_cols, kinds, *refs):
    refs = refs[3:]
    pieces = dict(zip(kinds, refs[: len(kinds)], strict=True))
    groups, out, planes, *states, result = refs[len(kinds) :]
    grid = (planes, *states)
    pair_count = pairs_of(box_rows)
    low_pair = pair_count - DEPTH // 2
    high_pair = SIDE // 2
    group = lax.axis_index("grp")
    box_x = lax.axis_index("box") % box_cols
    box_y = lax.axis_index("box") // box_cols

    def place_corner(piece, high_y, high_x):
        cells = piece[...].astype(F32)
        found = {(plane, dy): cells[row : row + run, :] for plane, dy, run, row in corner_runs()}
        for j in range(DEPTH // 2):
            k = (high_pair + j if high_y else low_pair + DEPTH // 2 - 1 - j) * XPOS
            near = [2 * j + 1, 2 * j + 2] if high_y else [2 * j + 2, 2 * j + 1]
            groups_of = []
            if (0, near[0]) in found:
                two = [normal([found[plane, dy] for plane in range(COEFS)]) for dy in near]
                groups_of += [(plane, low, high) for plane, (low, high) in enumerate(zip(*two, strict=True))]
            if (COEFS, 2 * j + 1) in found:
                pair = [found.get((COEFS, dy), jnp.zeros_like(found[COEFS, 2 * j + 1])) for dy in near]
                groups_of.append((7, *pair))
            for plane, low, high in groups_of:
                run = low.shape[0]
                x = SIDE if high_x else XPOS - run
                put_pair(grid, plane, pl.ds(k + x, run), odd_cells(run, x), low, high)

    for odd_y in (0, 1):
        for odd_x in (0, 1):

            @pl.when((box_y % 2 == odd_y) & (box_x % 2 == odd_x))
            def _():
                for (kind_y, kind_x), piece in pieces.items():
                    if None not in (kind_y, kind_x):
                        place_corner(piece, odd_y == kind_y, odd_x == kind_x)

    odd = odd_cells(XPOS, 0)

    def update(colour, k, count=XPOS):
        def at(offset):
            if isinstance(k, int):
                return pl.ds((k + offset) % pair_count * XPOS, count)
            return pl.ds(pl.multiple_of(lax.rem(k + (offset + pair_count), pair_count) * XPOS, XPOS), XPOS)

        wide = states[1 - colour][pl.ds(k * XPOS, XPOS) if count < XPOS else at(0), :]
        here = wide[:count]
        below = states[1 - colour][at(-1), :]
        above = states[1 - colour][at(1), :]
        if colour == 0:
            low, high = jnp.where(odd[:count], here, below), jnp.where(odd[:count], above, here)
        else:
            low, high = jnp.where(odd[:count], below, here), jnp.where(odd[:count], here, above)
        adjacent = (
            pltpu.roll(here, 1, 1),
            pltpu.roll(here, LANES - 1, 1),
            low,
            high,
            pltpu.roll(wide, 1, 0)[:count],
            pltpu.roll(wide, XPOS - 1, 0)[:count],
        )
        gathered = planes[colour, 6, at(0), :]
        for face in range(6):
            gathered = gathered + planes[colour, face, at(0), :] * adjacent[face]
        states[colour][at(0), :] = gathered

    even_row = box_y % 2 == 0
    for half_sweep in range(2 * SWEEPS):
        colour = half_sweep % 2
        for k in range(high_pair):
            update(colour, k, XPOS if half_sweep < DEPTH - 1 else SIDE)
        for j in range((DEPTH - half_sweep) // 2):
            if box_rows == 2:
                update(colour, jnp.where(even_row, high_pair + j, pair_count - 1 - j))
            else:
                update(colour, high_pair + j)
                update(colour, pair_count - 1 - j)

    odd = odd_cells(SIDE, 0)
    for half in range(2):
        cells = []
        for k in range(half * 4, half * 4 + 4):
            red = states[0][pl.ds(k * XPOS, SIDE), :]
            black = states[1][pl.ds(k * XPOS, SIDE), :]
            cells += [jnp.where(odd, black, red), jnp.where(odd, red, black)]
        result[pl.ds(0, LANES), pl.ds(half * LANES, LANES)] = jnp.concatenate(cells, axis=0).T
    count = jnp.int32(0)
    first = jnp.int32(0)
    for layer in range(groups.shape[0]):
        owner = groups[layer]
        count = count + jnp.where(owner == group, 1, 0)
        first = first + jnp.where(owner < group, 1, 0)
    start = pl.multiple_of(REACH + (first - group * LPD) * SIDE, 8)
    valid = lax.broadcasted_iota(jnp.int32, (OUT_ROWS, LANES), 0) < count * SIDE
    for half in range(2):
        value = result[pl.ds(start, OUT_ROWS), pl.ds(half * LANES, LANES)]
        out[pl.ds(half, OUT_ROWS, stride=2), :] = jnp.where(valid, value, 0.0)


def swaps(count, kind):
    pairs = []
    for low in range(kind, count - 1, 2):
        pairs += [(low, low + 1), (low + 1, low)]
    return pairs


def lateral_pairs(box_rows, box_cols, kind_y, kind_x):
    move_y = dict(swaps(box_rows, kind_y)) if kind_y is not None else {i: i for i in range(box_rows)}
    move_x = dict(swaps(box_cols, kind_x)) if kind_x is not None else {i: i for i in range(box_cols)}
    return [
        (y * box_cols + x, move_y[y] * box_cols + move_x[x])
        for y in range(box_rows)
        for x in range(box_cols)
        if y in move_y and x in move_x
    ]


def vmem(count):
    return [pl.BlockSpec(memory_space=pltpu.VMEM)] * count


def held(*arrays):
    return [pltpu.with_memory_space_constraint(array, pltpu.VMEM) for array in arrays]


def params():
    return pltpu.CompilerParams(vmem_limit_bytes=16 * 2**20)


def per_device(volume, apertures, conductivity, source, previous, cut_flags, new_group):
    group_count = lax.axis_size("grp")
    box_rows, box_cols = box_grid(lax.axis_size("box"))
    smem = pl.BlockSpec(memory_space=pltpu.SMEM)
    raw = (
        volume.reshape(ROWS, CELLS),
        apertures.reshape(6, ROWS, CELLS),
        conductivity.reshape(ROWS, CELLS),
        source.reshape(2 * ROWS, LANES),
        previous.reshape(2 * ROWS, LANES),
        cut_flags.T,
        new_group,
    )
    send_a, send_b, *local = pl.pallas_call(
        pack_kernel,
        out_shape=[pltpu.VMEM((10, REACH, CELLS), BF16)] * 2
        + [pltpu.VMEM(array.shape, array.dtype) for array in raw[:5]]
        + [pltpu.SMEM(array.shape, array.dtype) for array in raw[5:]],
        in_specs=[pl.BlockSpec(memory_space=pltpu.HBM)] * 7,
        out_specs=vmem(7) + [smem] * 2,
        scratch_shapes=[pltpu.SemaphoreType.DMA((7,))],
        compiler_params=params(),
        name="pack",
    )(*[pltpu.with_memory_space_constraint(array, pltpu.HBM) for array in raw])
    from_a = lax.ppermute(send_a, "grp", swaps(group_count, 0))
    from_b = lax.ppermute(send_b, "grp", swaps(group_count, 1))
    own = pl.pallas_call(
        own_kernel,
        out_shape=pltpu.VMEM((9, ROWS, CELLS), F32),
        in_specs=vmem(5) + [smem],
        out_specs=vmem(1)[0],
        compiler_params=params(),
        cost_estimate=pl.CostEstimate(flops=4 * 2**20, bytes_accessed=2**20, transcendentals=0),
        name="own",
    )(*held(*local[:5]), local[5])

    kinds_y = [0] if box_rows == 2 else [0, 1]
    kinds = [(kind, None) for kind in kinds_y] + [(None, 0), (None, 1)]
    kinds += [(kind_y, kind_x) for kind_y in kinds_y for kind_x in (0, 1)]
    shapes = [pltpu.VMEM((RIM if None in kind else CORNER, LANES), BF16) for kind in kinds]
    turned, *sends = pl.pallas_call(
        lambda *refs: turn_kernel(box_rows, box_cols, *refs),
        out_shape=[pltpu.VMEM((9, CELLS, LANES), F32)] + shapes[: len(kinds_y)],
        in_specs=vmem(3),
        out_specs=vmem(1 + len(kinds_y)),
        scratch_shapes=[pltpu.VMEM((LANES, CELLS), F32)],
        compiler_params=params(),
        name="turn",
    )(*held(own, from_a, from_b))
    sends += pl.pallas_call(
        lambda *refs: rims_kernel(box_rows, box_cols, *refs),
        out_shape=shapes[len(kinds_y) :],
        in_specs=vmem(1),
        out_specs=vmem(len(shapes) - len(kinds_y)),
        scratch_shapes=[pltpu.VMEM((CORNER, LANES), F32)],
        compiler_params=params(),
        cost_estimate=pl.CostEstimate(flops=2**20, bytes_accessed=2**20, transcendentals=0),
        name="rims",
    )(*held(turned))
    arrived = [
        lax.ppermute(send, "box", lateral_pairs(box_rows, box_cols, *kind))
        for send, kind in zip(sends, kinds, strict=True)
    ]
    sides = [array for array, kind in zip(arrived, kinds, strict=True) if None in kind]
    arrived = [array for array, kind in zip(arrived, kinds, strict=True) if None not in kind]
    kinds = [kind for kind in kinds if None not in kind]
    cells = pairs_of(box_rows) * XPOS
    grid_shapes = [pltpu.VMEM((2, COEFS - 1, cells, LANES), F32)] + [pltpu.VMEM((cells, LANES), F32)] * 2
    grid = pl.pallas_call(
        lambda *refs: prepare_kernel(box_rows, box_cols, *refs),
        out_shape=grid_shapes,
        in_specs=vmem(1),
        out_specs=vmem(3),
        compiler_params=params(),
        cost_estimate=pl.CostEstimate(flops=8 * 2**20, bytes_accessed=2**20, transcendentals=0),
        name="prepare",
    )(*held(turned))
    grid = pl.pallas_call(
        lambda *refs: sides_kernel(box_rows, box_cols, *refs),
        out_shape=grid_shapes,
        in_specs=vmem(3 + len(sides)),
        out_specs=vmem(3),
        input_output_aliases={0: 0, 1: 1, 2: 2},
        compiler_params=params(),
        cost_estimate=pl.CostEstimate(flops=2**10, bytes_accessed=2**10, transcendentals=0),
        name="sides",
    )(*held(*grid, *sides))
    smoothed, *_ = pl.pallas_call(
        lambda *refs: smooth_kernel(box_rows, box_cols, kinds, *refs),
        out_shape=[jax.ShapeDtypeStruct((2 * OUT_ROWS, LANES), F32)] + grid_shapes,
        in_specs=vmem(3 + len(kinds)) + [smem],
        out_specs=vmem(4),
        scratch_shapes=[pltpu.VMEM((REACH + SIDE + OUT_ROWS, CELLS), F32)],
        input_output_aliases={0: 1, 1: 2, 2: 3},
        compiler_params=params(),
        name="smooth",
    )(*held(*grid, *arrived), local[6])
    return smoothed.reshape(OUT_ROWS, 1, CELLS)


def solution(mesh):
    in_specs = (
        P("grp", "box", None),
        P(None, "grp", "box", None),
        P("grp", "box", None),
        P("grp", "box", None),
        P("grp", "box", None),
        P(),
        P(),
    )
    out_specs = P("grp", "box", None)
    return jax.shard_map(
        per_device, mesh=mesh, in_specs=in_specs, out_specs=out_specs, check_vma=False
    )
```
